512 devices in a mesh: snap: 4 (over y_lo), gx: 16 (over z, core), gy: 8 (over y_hi, x).
Axes of the slice: x: 4, y: 8 (y_hi: 2, y_lo: 4; y = y_hi * 4 + y_lo), z: 8, core: 2. Of those that a mesh axis runs over, the one named last changes fastest.
Arguments:
- displacements: float32 [64, 3, 64, 1024], P('snap', None, 'gx', 'gy')
- forces: float32 [64, 3, 64, 1024], P('snap', None, 'gx', 'gy')
- neighbours: int32 [8, 64, 1024], P(None, 'gx', 'gy'), may hold values 0 or 1
- species: int32 [64, 1024], P('gx', 'gy'), may hold values from 0 to 2
- block_of: int32 [64, 1024], P('gx', 'gy'), may hold values from 0 to 3, as said below
- precond: float32 [512, 3, 24, 24], P(('gx', 'gy')), may hold values from -0.1 to 0.8, as said below
- vectors: float32 [256, 3, 64, 1024], P('snap', None, 'gx', 'gy'), may hold values from -6 to 6
Outputs:
- constants: float32 [512, 3, 24, 3], P(('gx', 'gy'))
- chebyshev: float32 [256, 3, 64, 1024], P('snap', None, 'gx', 'gy')
The draws below stay inside these ranges and needn't reach their ends.
Inputs may be any that keep to these rules, and one draw needn't show every extreme that they name: `block_of`: on each device's 4 x 128 atoms, every block index holds exactly 128 atoms. `precond`: each matrix has its diagonal between 0.4 and 0.8 and small off-diagonal entries.
All inputs are finite; a program needn't handle non-finite values. No bound on the sum of `neighbours` on one device may be relied on, other than what follows from the above.
Results may differ from the reference program's by a relative error of at most 0.00011.
Values sent between devices are 32-bit elements; how exact they have to be, the bound alone decides.
No kernel may reach another device: no remote copies, remote signals or barrier semaphores. Data moves between devices by JAX's collectives and lax.ppermute only.
A program may use at most 64 MiB of HBM per device.

```python
import jax
import jax.numpy as jnp
from jax import lax

AX = 4
AY = 128
AB = 128
NSPEC = 3
NOFF = 8
P_SIZE = 24
BLK_DEV = 4
NBLK = 512
GXA = 64
GYA = 1024
SNAPS = 64
NV = 256


def joint_fields(key):
    base = jax.random.fold_in(key, 11)
    key_disp, key_stiff, key_noise = jax.random.split(base, 3)
    shape = (SNAPS, 3, GXA, GYA)
    moves = jax.random.normal(key_disp, shape, jnp.float32)
    stiff = jnp.exp(jax.random.uniform(key_stiff, (1, 3, GXA, GYA), jnp.float32, -0.7, 0.7))
    noise = jax.random.normal(key_noise, shape, jnp.float32)
    return (moves, -stiff * moves + 0.3 * noise)


def draw_displacements(key, part):
    return joint_fields(key)[0]


def draw_forces(key, part):
    return joint_fields(key)[1]


def draw_block_of(key, part):
    count_x = GXA // AX
    count_y = GYA // AY
    keys = jax.random.split(jax.random.fold_in(key, 23), count_x * count_y)
    perms = jax.vmap(lambda single: jax.random.permutation(single, AX * AY))(keys)
    blocks = (perms // AB).astype(jnp.int32).reshape(count_x, count_y, AX, AY)
    return blocks.transpose(0, 2, 1, 3).reshape(GXA, GYA)


def draw_precond(key, part):
    key_diag, key_off = jax.random.split(jax.random.fold_in(key, 37), 2)
    diag = jax.random.uniform(key_diag, (NBLK, NSPEC, P_SIZE), jnp.float32, 0.4, 0.8)
    off = jax.random.uniform(key_off, (NBLK, NSPEC, P_SIZE, P_SIZE), jnp.float32, -1.0, 1.0) * 0.1
    eye = jnp.eye(P_SIZE, dtype=jnp.float32)
    return off * (1.0 - eye) + eye * diag[..., None]


def touch_ends(values, stream_key, low, top_value):
    extent = values.shape
    spot = [jax.random.randint(jax.random.fold_in(stream_key, axis), (), 0, extent[axis]) for axis in range(len(extent))]
    values = values.at[tuple(spot)].set(low)
    longest = extent.index(max(extent))
    spot[longest] = (spot[longest] + 1) % extent[longest]
    return values.at[tuple(spot)].set(top_value)


def shard_levels(stream_key, shape, pieces, low, largest):
    factor_of, own = 1.0, jax.random.fold_in(stream_key, 6)
    for position, shards_of in pieces:
        heights = jnp.exp(jax.random.uniform(jax.random.fold_in(own, position), (shards_of,), jnp.float32, low / len(pieces), largest / len(pieces)))
        factor_of = factor_of * jnp.repeat(heights, shape[position] // shards_of).reshape([-1 if axis == position else 1 for axis in range(len(shape))])
    return factor_of


def gaussian(rng, shape, width, most, cuts=(), kind=jnp.bfloat16):
    level = shard_levels(rng, shape, cuts, -0.22, 0.18) if cuts else 1.0
    drawn = jax.random.normal(rng, shape, jnp.float32) * width * level
    return jnp.minimum(jnp.maximum(drawn, -most), most).astype(kind)


def setup_inputs(seed: int = 0) -> dict:
    splits = jax.random.split(jax.random.key(seed), 8)
    return {
        "displacements": draw_displacements(jax.random.fold_in(splits[7], 71), 0),
        "forces": draw_forces(jax.random.fold_in(splits[7], 71), 0),
        "neighbours": touch_ends((jax.random.randint(splits[2], (NOFF, GXA, GYA), 0, 4) < 3).astype(jnp.int32), jax.random.fold_in(splits[2], 1), 0, 1),
        "species": touch_ends(jax.random.randint(splits[3], (GXA, GYA), 0, NSPEC), jax.random.fold_in(splits[3], 1), 0, NSPEC - 1).astype(jnp.int32),
        "block_of": draw_block_of(jax.random.fold_in(splits[7], 71), 0),
        "precond": draw_precond(jax.random.fold_in(splits[7], 71), 0),
        "vectors": gaussian(splits[6], (NV, 3, GXA, GYA), 1.0, 6.0, ((0, 4), (2, 16), (3, 8)), jnp.float32),
    }


offsets = ((-1, -1), (-1, 0), (-1, 1), (0, -1), (0, 1), (1, -1), (1, 0), (1, 1))


def moved_field(field, step_x, step_y):
    return jnp.roll(field, (-step_x, -step_y), axis=(2, 3))


def apply_operator(field, weights):
    result = jnp.zeros_like(field)
    for index, (step_x, step_y) in enumerate(offsets):
        differ = moved_field(field, step_x, step_y) - field
        result = result - jnp.sum(differ[:, :, None] * weights[index][None], axis=1)
    return result


def refine(precond, gram, rhs):
    high = lax.Precision.HIGHEST
    first = jnp.einsum('gpq,gqa->gpa', precond, rhs, precision=high)
    remain = rhs - jnp.einsum('gpq,gqa->gpa', gram, first, precision=high)
    return first + jnp.einsum('gpq,gqa->gpa', precond, remain, precision=high)


def reference(displacements, forces, neighbours, species, block_of, precond, vectors):
    high = lax.Precision.HIGHEST
    mask = neighbours.astype(jnp.float32)
    parts = []
    for index, (step_x, step_y) in enumerate(offsets):
        parts.append((moved_field(displacements, step_x, step_y) - displacements) * mask[index][None, None])
    feats = jnp.stack(parts, 1).reshape(SNAPS, P_SIZE, GXA * GYA)
    loads = forces.reshape(SNAPS, 3, GXA * GYA)
    rows_idx = jnp.arange(GXA, dtype=jnp.int32)[:, None]
    cols_idx = jnp.arange(GYA, dtype=jnp.int32)[None, :]
    device_id = (rows_idx // AX) * (GYA // AY) + cols_idx // AY
    group = ((device_id * BLK_DEV + block_of) * NSPEC + species).reshape(GXA * GYA).astype(jnp.int32)
    n_groups = NBLK * NSPEC
    pair = jnp.einsum('spi,sqi->ipq', feats, feats, precision=high).reshape(GXA * GYA, P_SIZE * P_SIZE)
    cross = jnp.einsum('spi,sai->ipa', feats, loads, precision=high).reshape(GXA * GYA, P_SIZE * 3)
    scale = 1.0 / (SNAPS * AB)
    gram = jax.ops.segment_sum(pair, group, num_segments=n_groups).reshape(n_groups, P_SIZE, P_SIZE) * scale
    rhs = jax.ops.segment_sum(cross, group, num_segments=n_groups).reshape(n_groups, P_SIZE, 3) * scale
    theta = refine(precond.reshape(n_groups, P_SIZE, P_SIZE), gram, rhs)
    per_atom = theta.reshape(n_groups, P_SIZE * 3)[group]
    weights = per_atom.T.reshape(NOFF, 3, 3, GXA, GYA) * mask[:, None, None]
    first_term = apply_operator(vectors, weights)
    chebyshev = 2.0 * apply_operator(first_term, weights) - vectors
    return theta.reshape(NBLK, NSPEC, P_SIZE, 3), chebyshev
```

```python
import functools

import jax
import jax.numpy as jnp
from jax import lax
from jax.experimental import pallas as pl
from jax.experimental.pallas import tpu as pltpu
from jax.sharding import PartitionSpec as P

AB = 128
NSPEC = 3
OFFSETS = ((-1, -1), (-1, 0), (-1, 1), (0, -1), (0, 1), (1, -1), (1, 0), (1, 1))
NG = 12
NP = 24
HIGH = lax.Precision.HIGHEST
F32 = jnp.float32


def lanes_of(shape):
    return lax.broadcasted_iota(jnp.int32, shape, 1)


def subs_of(shape):
    return lax.broadcasted_iota(jnp.int32, shape, 0)


def lane_slot(slot, k):
    return slot // 5, (slot % 5) * 18 + k


def pack_columns(even, tile_at, slots, near_ref, far_ref):
    lane = lanes_of((8, 128))
    for t in range(2):
        first = jnp.zeros((8, 128), F32)
        last = jnp.zeros((8, 128), F32)
        for slot in slots:
            for k in range(18):
                tile, at = lane_slot(slot, k)
                if tile != t:
                    continue
                here = lane == at
                values = tile_at(slot, k)
                first = jnp.where(here, pltpu.roll(values, at, 1) if at else values, first)
                last = jnp.where(here, pltpu.roll(values, (at + 1) % 128, 1), last)
        rows = pl.ds(8 * t, 8)
        near_ref[rows, :] = jnp.where(even, last, first)
        far_ref[rows, :] = jnp.where(even, first, last)


def spread_columns(even, tile_at, slots, near_ref, far_ref, shift_ref, height):
    lane = lanes_of((8, 128))
    from_left, from_right = [], []
    for t in range(2):
        near, far = near_ref[pl.ds(8 * t, 8), :], far_ref[pl.ds(8 * t, 8), :]
        from_left.append(jnp.where(even, far, near))
        from_right.append(jnp.where(even, near, far))
    for k in range(18):
        for place, slot in enumerate(slots):
            tile, at = lane_slot(slot, k)
            values = tile_at(slot, k)
            edge_left = pltpu.roll(from_left[tile], (128 - at) % 128, 1) if at else from_left[tile]
            edge_right = pltpu.roll(from_right[tile], (127 - at) % 128, 1)
            base = k * height + 8 * place
            shift_ref[pl.ds(base, 8), :] = jnp.where(lane == 0, edge_left, pltpu.roll(values, 1, 1))
            shift_ref[pl.ds(18 * height + base, 8), :] = values
            shift_ref[pl.ds(36 * height + base, 8), :] = jnp.where(lane == 127, edge_right, pltpu.roll(values, 127, 1))


def rows_kernel(par, disp, vec, core, other):
    even = par[0] == 0
    for b in range(3):
        for source, count, base in ((disp, 16, 0), (vec, 64, 48)):
            low = source[pl.ds(4 * b, count, stride=12), :]
            high = source[pl.ds(4 * b + 3, count, stride=12), :]
            at = pl.ds(base + b * count, count)
            core[at, :] = jnp.where(even, high, low)
            other[at, :] = jnp.where(even, low, high)


def natural_tile(source, count, core, other, base, even):
    def tile(place, k):
        b, x = k // 6, k % 6 - 1
        if 0 <= x < 4:
            return source[pl.ds(12 * 8 * place + 4 * b + x, 8, stride=12), :]
        at = pl.ds(base + b * count + 8 * place, 8)
        return jnp.where(even, other[at, :], core[at, :]) if x < 0 else jnp.where(even, core[at, :], other[at, :])

    return tile


def blocked_tile(source, core, other, even):
    def tile(place, k):
        b, x = k // 6, k % 6 - 1
        if 0 <= x < 4:
            return source[pl.ds((4 * b + x) * 64 + 8 * place, 8), :]
        at = pl.ds(b * 64 + 8 * place, 8)
        return jnp.where(even, other[at, :], core[at, :]) if x < 0 else jnp.where(even, core[at, :], other[at, :])

    return tile


def columns_kernel(par, disp, vec, core, other, near, far):
    even = par[0] == 0
    disp_tile = natural_tile(disp, 16, core, other, 0, even)
    vec_tile = natural_tile(vec, 64, core, other, 48, even)
    pack_columns(
        par[1] == 0,
        lambda slot, k: disp_tile(slot, k) if slot < 2 else vec_tile(slot - 2, k),
        range(10),
        near,
        far,
    )


def term_columns_kernel(par, term, core, other, near, far):
    tile = blocked_tile(term, core, other, par[0] == 0)
    pack_columns(par[1] == 0, tile, range(8), near, far)


def fold_rows(tiles, sub):
    for bit in (1, 2, 4):
        low = (sub & bit) == 0
        tiles = [
            jnp.where(low, tiles[2 * i], tiles[2 * i + 1])
            + pltpu.roll(jnp.where(low, tiles[2 * i + 1], tiles[2 * i]), bit, 0)
            for i in range(len(tiles) // 2)
        ]
    return tiles[0]


def fold_lanes(tiles, quarter):
    for bit in (1, 2):
        low = (quarter & bit) == 0
        tiles = [
            jnp.where(low, tiles[2 * i], tiles[2 * i + 1])
            + pltpu.roll(jnp.where(low, tiles[2 * i + 1], tiles[2 * i]), 32 * bit, 1)
            for i in range(len(tiles) // 2)
        ]
    return tiles[0]


PAIRS = [(q, p) for q in range(NP) for p in range(q, NP + 3)]
PAIR_AT = {pair: i for i, pair in enumerate(PAIRS)}
PAYLOAD = 168
CHUNK = 62


def gram_kernel(copies, par, disp, forces, nbr, species, block_of, core, other, near, far, out, shift, feats, sums):
    tile = natural_tile(disp, 16, core, other, 0, par[0] == 0)
    spread_columns(par[1] == 0, tile, range(2), near, far, shift, 16)
    for x in range(4):
        for o, (dx, dy) in enumerate(OFFSETS):
            mask = nbr[pl.ds(4 * o + x, 1), :].astype(F32)
            for b in range(3):
                moved = shift[pl.ds(((dy + 1) * 18 + 6 * b + x + dx + 1) * 16, 16), :]
                center = shift[pl.ds((18 + 6 * b + x + 1) * 16, 16), :]
                feats[pl.ds((3 * o + b) * 64 + x, 16, stride=4), :] = (moved - center) * mask
        for a in range(3):
            feats[pl.ds((NP + a) * 64 + x, 16, stride=4), :] = forces[pl.ds(4 * a + x, 16, stride=12), :]
    for q in range(NP):
        left = feats[pl.ds(q * 64, 64), :].reshape(8, 8, 128)
        for p in range(q, NP + 3):
            right = feats[pl.ds(p * 64, 64), :].reshape(8, 8, 128)
            sums[pl.ds(PAIR_AT[q, p] * 8, 8), :] = jnp.sum(left * right, axis=0)
    group = block_of[...] * NSPEC + species[...]
    which = subs_of((32, 128))
    members = jnp.concatenate([(which == group[x : x + 1, :]).astype(F32) for x in range(4)], axis=0)
    members = members.astype(jnp.bfloat16)
    members = jnp.concatenate([members, members], axis=1)
    sub, quarter = subs_of((8, 128)), lanes_of((8, 128)) // 32
    own = ((sub & 3) == quarter).astype(F32)
    for c in range(len(PAIRS) // CHUNK):
        at = pl.ds(c * CHUNK * 8, CHUNK * 8)
        value = sums[at, :]
        high = value.astype(jnp.bfloat16)
        low = (value - high.astype(F32)).astype(jnp.bfloat16)
        by_group = lax.dot_general(
            jnp.concatenate([high, low], axis=1), members, (((1,), (1,)), ((), ())), preferred_element_type=F32
        )
        sums[at, :] = (by_group.reshape(CHUNK, 8, 128) * own[None]).reshape(CHUNK * 8, 128)

    def entry(q, p):
        return sums[pl.ds(PAIR_AT[min(q, p), max(q, p)] * 8, 8), :]

    packed = []
    for first in range(0, 72, 4):
        packed.append(
            fold_lanes(
                [fold_rows([entry(i // 3, 8 * (i % 3) + r) for r in range(8)], sub) for i in range(first, first + 4)],
                quarter,
            )
        )
    for block in range(3):
        tiles = [fold_rows([entry(8 * block + r, NP + a) for r in range(8)], sub) for a in range(3)]
        packed.append(fold_lanes(tiles + [jnp.zeros((8, 128), F32)], quarter))
    for i, value in enumerate(packed):
        for copy in range(copies):
            out[pl.ds(copy * PAYLOAD + 8 * i, 8), :] = value


def apply_operator(shift, weights, height, emit):
    for x in range(4):
        total = [None] * 3
        for b in range(3):
            center = shift[pl.ds((18 + 6 * b + x + 1) * height, height), :]
            for o, (dx, dy) in enumerate(OFFSETS):
                moved = shift[pl.ds(((dy + 1) * 18 + 6 * b + x + dx + 1) * height, height), :]
                differ = center - moved
                for a in range(3):
                    term = differ * weights[pl.ds(72 * x + 24 * a + 3 * o + b, 1), :]
                    total[a] = term if total[a] is None else total[a] + term
        for a in range(3):
            emit(a, x, total[a])


def fit_kernel(
    copies, scale, par, sums, precond, vec, nbr, species, block_of, core, other, near, far,
    theta, weights, term, core_out, other_out, shift, gram,
):
    lane = lanes_of((8, 128))
    quarter = lane // 32

    def total(i):
        value = sums[pl.ds(8 * i, 8), :]
        for copy in range(1, copies):
            value = value + sums[pl.ds(copy * PAYLOAD + 8 * i, 8), :]
        return value * scale

    for m in range(18):
        value = total(m)
        for k in range(4):
            part = jnp.where(quarter == k, value, 0.0)
            part = part + pltpu.roll(part, 32, 1)
            gram[pl.ds(8 * (4 * m + k), 8), :] = part + pltpu.roll(part, 64, 1)
    rhs = jnp.concatenate([total(18 + i) for i in range(3)], axis=0)
    of_group = lanes_of((NP, 128)) & 31

    def solve(right):
        every = jnp.dot(precond[...], right, precision=HIGH, preferred_element_type=F32)
        result = every[0:NP]
        for g in range(1, NG):
            result = jnp.where(of_group == g, every[g * NP : (g + 1) * NP], result)
        return result

    first = solve(rhs)
    remain = rhs
    for q in range(NP):
        remain = remain - gram[pl.ds(NP * q, NP), :] * first[q : q + 1, :]
    fitted = first + solve(remain)
    theta[...] = fitted

    of_part = lanes_of((NP, 128)) // 32
    stacked = jnp.concatenate(
        [jnp.where((of_part == a) & (of_group < NG), fitted, 0.0) for a in range(3)], axis=0
    )
    group = block_of[...] * NSPEC + species[...]
    which = subs_of((128, 128)) & 31
    p_row, o_col = subs_of((NP, 8)), lanes_of((NP, 8))
    repeat = ((p_row >= 3 * o_col) & (p_row < 3 * o_col + 3)).astype(F32)
    for x in range(4):
        member = (which == group[x : x + 1, :]).astype(F32)
        by_atom = jnp.dot(stacked, member, precision=HIGH, preferred_element_type=F32)
        mask = nbr[pl.ds(x, 8, stride=4), :].astype(F32)
        mask = jnp.dot(repeat, mask, precision=HIGH, preferred_element_type=F32)
        weights[pl.ds(72 * x, 72), :] = by_atom * jnp.concatenate([mask, mask, mask], axis=0)

    even = par[0] == 0
    tile = natural_tile(vec, 64, core, other, 48, even)
    spread_columns(par[1] == 0, lambda slot, k: tile(slot - 2, k), range(2, 10), near, far, shift, 64)

    edge = {}

    def emit(a, x, value):
        term[pl.ds((4 * a + x) * 64, 64), :] = value
        if x == 0:
            core_out[pl.ds(64 * a, 64), :] = value
            other_out[pl.ds(64 * a, 64), :] = value
        if x == 3:
            at = pl.ds(64 * a, 64)
            low = core_out[at, :]
            core_out[at, :] = jnp.where(even, value, low)
            other_out[at, :] = jnp.where(even, low, value)

    apply_operator(shift, weights, 64, emit)


def last_kernel(par, term, core, other, near, far, weights, vec, out, shift):
    tile = blocked_tile(term, core, other, par[0] == 0)
    spread_columns(par[1] == 0, tile, range(8), near, far, shift, 64)

    def emit(a, x, value):
        at = pl.ds(4 * a + x, 64, stride=12)
        out[at, :] = 2.0 * value - vec[at, :]

    apply_operator(shift, weights, 64, emit)


def call(kernel, name, n_in, outs, scratch=()):
    in_vmem = pl.BlockSpec(memory_space=pltpu.VMEM)
    return pl.pallas_call(
        kernel,
        name=name,
        in_specs=[pl.BlockSpec(memory_space=pltpu.SMEM)] + [in_vmem] * n_in,
        out_specs=[in_vmem] * len(outs),
        out_shape=[jax.ShapeDtypeStruct((rows, 128), F32) for rows in outs],
        scratch_shapes=[pltpu.VMEM((rows, 128), F32) for rows in scratch],
        compiler_params=pltpu.CompilerParams(vmem_limit_bytes=40 << 20),
    )


def swap(value, axis, odd):
    n = lax.axis_size(axis)
    if odd:
        pairs = [(i, (i + 1) % n) for i in range(1, n, 2)]
        pairs += [((i + 1) % n, i) for i in range(1, n, 2)]
    else:
        pairs = [(i, i ^ 1) for i in range(n)]
    return lax.ppermute(value, axis, pairs)


def shards(displacements, forces, neighbours, species, block_of, precond, vectors):
    snap = lax.axis_size("snap")
    scale = 1.0 / (displacements.shape[0] * snap * AB)
    disp = displacements.reshape(-1, 128)
    load = forces.reshape(-1, 128)
    vec = vectors.reshape(-1, 128)
    nbr = neighbours.reshape(-1, 128)
    par = jnp.stack([lax.axis_index("gx") % 2, lax.axis_index("gy") % 2]).astype(jnp.int32)

    core, other = call(rows_kernel, "rows", 2, (240, 240))(par, disp, vec)
    core, other = swap(core, "gx", False), swap(other, "gx", True)
    near, far = call(columns_kernel, "columns", 4, (16, 16))(par, disp, vec, core, other)
    far, near = swap(far, "gy", True), swap(near, "gy", False)
    (part,) = call(
        functools.partial(gram_kernel, snap), "gram", 9, (snap * PAYLOAD,), (54 * 16, 27 * 64, len(PAIRS) * 8)
    )(par, disp, load, nbr, species, block_of, core, other, near, far)
    part = lax.all_to_all(part, "snap", 0, 0, tiled=True)
    theta, weights, term, core2, other2 = call(
        functools.partial(fit_kernel, snap, scale), "fit", 10, (NP, 288, 768, 192, 192), (54 * 64, 576)
    )(par, part, precond.reshape(NG * NP, NP), vec, nbr, species, block_of, core, other, near, far)
    core2, other2 = swap(core2, "gx", False), swap(other2, "gx", True)
    near2, far2 = call(term_columns_kernel, "term_columns", 3, (16, 16))(par, term, core2, other2)
    far2, near2 = swap(far2, "gy", True), swap(near2, "gy", False)
    (result,) = call(last_kernel, "last", 7, (768,), (54 * 64,))(par, term, core2, other2, near2, far2, weights, vec)

    constants = theta.reshape(NP, 4, 32)[:, :3, :NG].transpose(2, 0, 1)
    return (
        constants.reshape(precond.shape[0], precond.shape[1], NP, 3),
        result.reshape(vectors.shape),
    )


def solution(mesh):
    in_specs = (
        P("snap", None, "gx", "gy"),
        P("snap", None, "gx", "gy"),
        P(None, "gx", "gy"),
        P("gx", "gy"),
        P("gx", "gy"),
        P(("gx", "gy"), None, None, None),
        P("snap", None, "gx", "gy"),
    )
    out_specs = (P(("gx", "gy"), None, None, None), P("snap", None, "gx", "gy"))
    return jax.shard_map(shards, mesh=mesh, in_specs=in_specs, out_specs=out_specs, check_vma=False)
```

```python
import functools

import jax
import jax.numpy as jnp
from jax import lax
from jax.experimental import pallas as pl
from jax.experimental.pallas import tpu as pltpu
from jax.sharding import PartitionSpec as P

AB = 128
NSPEC = 3
OFFSETS = ((-1, -1), (-1, 0), (-1, 1), (0, -1), (0, 1), (1, -1), (1, 0), (1, 1))
NG = 12
NP = 24
HIGH = lax.Precision.HIGHEST
F32 = jnp.float32


def lanes_of(shape):
    return lax.broadcasted_iota(jnp.int32, shape, 1)


def subs_of(shape):
    return lax.broadcasted_iota(jnp.int32, shape, 0)


def lane_slot(slot, k):
    return slot // 3, (slot % 3) * 36 + 2 * k


def pack_columns(tile_at, slots, columns):
    pair = lanes_of((8, 128)) // 2
    packed = [jnp.zeros((8, 128), F32) for _ in range(columns.shape[0] // 8)]
    for slot in slots:
        for k in range(18):
            t, at = lane_slot(slot, k)
            packed[t] = jnp.where(pair == at // 2, pltpu.roll(tile_at(slot, k), (at + 1) % 128, 1), packed[t])
    for t, value in enumerate(packed):
        columns[pl.ds(8 * t, 8), :] = value


def spread_columns(even, tile_at, slots, near_ref, far_ref, shift_ref, height):
    lane = lanes_of((8, 128))
    edges = {}
    for t in sorted({lane_slot(slot, 0)[0] for slot in slots}):
        near, far = near_ref[pl.ds(8 * t, 8), :], far_ref[pl.ds(8 * t, 8), :]
        left, right = jnp.where(even, far, near), jnp.where(even, near, far)
        edges[t] = jnp.where((lane & 1) == 0, pltpu.roll(right, 127, 1), pltpu.roll(left, 1, 1))
    for k in range(18):
        for place, slot in enumerate(slots):
            t, at = lane_slot(slot, k)
            values = tile_at(slot, k)
            edge = pltpu.roll(edges[t], 127 - at, 1)
            base = k * height + 8 * place
            shift_ref[pl.ds(base, 8), :] = jnp.where(lane == 0, edge, pltpu.roll(values, 1, 1))
            shift_ref[pl.ds(18 * height + base, 8), :] = values
            shift_ref[pl.ds(36 * height + base, 8), :] = jnp.where(lane == 127, edge, pltpu.roll(values, 127, 1))


def rows_kernel(disp, vec, low, high, sems):
    copies = []
    for out, x in ((low, 0), (high, 3)):
        for source, at in ((disp, pl.ds(0, 48)), (vec, pl.ds(48, 192))):
            copies.append(pltpu.make_async_copy(source.at[:, x, :], out.at[at, :], sems.at[len(copies)]))
    for copy in copies:
        copy.start()
    for copy in copies:
        copy.wait()


def natural_tile(source, above, below, base):
    def tile(place, k):
        b, x = k // 6, k % 6 - 1
        if 0 <= x < 4:
            return source[pl.ds(12 * 8 * place + 4 * b + x, 8, stride=12), :]
        return (above if x < 0 else below)[pl.ds(base + 24 * place + b, 8, stride=3), :]

    return tile


def blocked_tile(source, above, below):
    def tile(place, k):
        b, x = k // 6, k % 6 - 1
        if 0 <= x < 4:
            return source[pl.ds((4 * b + x) * 64 + 8 * place, 8), :]
        return (above if x < 0 else below)[pl.ds(b * 64 + 8 * place, 8), :]

    return tile


def columns_kernel(disp, vec, above, below, columns):
    disp_tile = natural_tile(disp, above, below, 0)
    vec_tile = natural_tile(vec, above, below, 48)
    pack_columns(lambda slot, k: disp_tile(slot, k) if slot < 2 else vec_tile(slot - 2, k), range(10), columns)


def term_columns_kernel(term, above, below, columns):
    pack_columns(blocked_tile(term, above, below), range(8), columns)


def fold_rows(tiles, sub):
    for bit in (1, 2, 4):
        low = (sub & bit) == 0
        tiles = [
            jnp.where(low, tiles[2 * i], tiles[2 * i + 1])
            + pltpu.roll(jnp.where(low, tiles[2 * i + 1], tiles[2 * i]), bit, 0)
            for i in range(len(tiles) // 2)
        ]
    return tiles[0]


def fold_lanes(tiles, eighth):
    for bit in (1, 2, 4):
        low = (eighth & bit) == 0
        tiles = [
            jnp.where(low, tiles[2 * i], tiles[2 * i + 1])
            + pltpu.roll(jnp.where(low, tiles[2 * i + 1], tiles[2 * i]), 16 * bit, 1)
            for i in range(len(tiles) // 2)
        ]
    return tiles[0]


PAIRS = [(q, p) for q in range(NP) for p in range(q, NP + 3)]
PAIR_AT = {pair: i for i, pair in enumerate(PAIRS)}
BLOCKS = [(i, j) for i in range(3) for j in range(i, 3)]
PAYLOAD = 64
CHUNK = 62


def gram_kernel(copies, par, disp, forces, nbr, species, block_of, above, below, far, near, out, shift, feats, sums):
    tile = natural_tile(disp, above, below, 0)
    spread_columns(par[0] == 0, tile, range(2), near, far, shift, 16)
    for x in range(4):
        for o, (dx, dy) in enumerate(OFFSETS):
            mask = nbr[pl.ds(4 * o + x, 1), :].astype(F32)
            for b in range(3):
                moved = shift[pl.ds(((dy + 1) * 18 + 6 * b + x + dx + 1) * 16, 16), :]
                center = shift[pl.ds((18 + 6 * b + x + 1) * 16, 16), :]
                feats[pl.ds((3 * o + b) * 64 + x, 16, stride=4), :] = (moved - center) * mask
        for a in range(3):
            feats[pl.ds((NP + a) * 64 + x, 16, stride=4), :] = forces[pl.ds(4 * a + x, 16, stride=12), :]
    for q in range(NP):
        left = feats[pl.ds(q * 64, 64), :].reshape(8, 8, 128)
        for p in range(q, NP + 3):
            right = feats[pl.ds(p * 64, 64), :].reshape(8, 8, 128)
            sums[pl.ds(PAIR_AT[q, p] * 8, 8), :] = jnp.sum(left * right, axis=0)
    group = block_of[...] * NSPEC + species[...]
    which = subs_of((16, 128))
    members = jnp.concatenate([(which == group[x % 4 : x % 4 + 1, :]).astype(F32) for x in range(8)], axis=0)
    members = members.astype(jnp.bfloat16)
    members = jnp.concatenate([members, members], axis=1)
    sub, eighth = subs_of((8, 128)), lanes_of((8, 128)) // 16
    own = (sub == eighth).astype(F32)
    for c in range(len(PAIRS) // CHUNK):
        at = pl.ds(c * CHUNK * 8, CHUNK * 8)
        value = sums[at, :]
        high = value.astype(jnp.bfloat16)
        low = (value - high.astype(F32)).astype(jnp.bfloat16)
        by_group = lax.dot_general(
            jnp.concatenate([high, low], axis=1), members, (((1,), (1,)), ((), ())), preferred_element_type=F32
        )
        sums[at, :] = (by_group.reshape(CHUNK, 8, 128) * own[None]).reshape(CHUNK * 8, 128)

    def column(fixed, block):
        pairs = [(min(fixed, 8 * block + r), max(fixed, 8 * block + r)) for r in range(8)]
        return fold_rows([sums[pl.ds(PAIR_AT[pair] * 8, 8), :] for pair in pairs], sub)

    packed = [fold_lanes([column(8 * i + r, j) for r in range(8)], eighth) for i, j in BLOCKS]
    sides = [column(NP + a, block) for a in range(3) for block in range(3)] + [jnp.zeros((8, 128), F32)] * 7
    packed += [fold_lanes(sides[:8], eighth), fold_lanes(sides[8:], eighth)]
    for i, value in enumerate(packed):
        for copy in range(copies):
            out[pl.ds(copy * PAYLOAD + 8 * i, 8), :] = value


def apply_operator(shift, weights, height, emit):
    for x in range(4):
        total = [None] * 3
        for b in range(3):
            center = shift[pl.ds((18 + 6 * b + x + 1) * height, height), :]
            for o, (dx, dy) in enumerate(OFFSETS):
                moved = shift[pl.ds(((dy + 1) * 18 + 6 * b + x + dx + 1) * height, height), :]
                differ = center - moved
                for a in range(3):
                    term = differ * weights[pl.ds(72 * x + 24 * a + 3 * o + b, 1), :]
                    total[a] = term if total[a] is None else total[a] + term
        for a in range(3):
            emit(a, x, total[a])


def fit_kernel(
    copies, scale, par, sums, precond, vec, nbr, species, block_of, above, below, far, near,
    theta, weights, term, low_out, high_out, shift,
):
    sub, eighth = subs_of((8, 128)), lanes_of((8, 128)) // 16

    def total(i):
        value = sums[pl.ds(8 * i, 8), :]
        for copy in range(1, copies):
            value = value + sums[pl.ds(copy * PAYLOAD + 8 * i, 8), :]
        return value * scale

    def spread(value, k):
        value = jnp.where(eighth == k, value, 0.0)
        for step in (16, 32, 64):
            value = value + pltpu.roll(value, step, 1)
        return value

    sides = [spread(total(6 + i // 8), i % 8) for i in range(9)]
    rhs = []
    for block in range(3):
        value = jnp.where(eighth == 0, sides[block], 0.0)
        for a in (1, 2):
            value = jnp.where(eighth == a, sides[3 * a + block], value)
        rhs.append(value)
    of_group = lanes_of((NP, 128)) & 15

    def solve(right):
        every = jnp.dot(precond[...], right, precision=HIGH, preferred_element_type=F32)
        result = every[0:NP]
        for g in range(1, NG):
            result = jnp.where(of_group == g, every[g * NP : (g + 1) * NP], result)
        return result

    first = solve(jnp.concatenate(rhs, axis=0))
    part = [first[8 * i : 8 * i + 8] for i in range(3)]
    remain = list(rhs)
    for m, (i, j) in enumerate(BLOCKS):
        value = total(m)
        tiles = [spread(value, r) for r in range(8)]
        for r in range(8):
            remain[j] = remain[j] - tiles[r] * part[i][r : r + 1, :]
        if i != j:
            remain[i] = remain[i] - fold_rows([tiles[r] * part[j] for r in range(8)], sub)
    fitted = first + solve(jnp.concatenate(remain, axis=0))
    theta[...] = fitted

    of_part = lanes_of((NP, 128)) // 16
    stacked = jnp.concatenate(
        [jnp.where((of_part == a) & (of_group < NG), fitted, 0.0) for a in range(3)], axis=0
    )
    group = block_of[...] * NSPEC + species[...]
    which = subs_of((128, 128)) & 15
    p_row, o_col = subs_of((NP, 8)), lanes_of((NP, 8))
    repeat = ((p_row >= 3 * o_col) & (p_row < 3 * o_col + 3)).astype(F32)
    for x in range(4):
        member = (which == group[x : x + 1, :]).astype(F32)
        by_atom = jnp.dot(stacked, member, precision=HIGH, preferred_element_type=F32)
        mask = nbr[pl.ds(x, 8, stride=4), :].astype(F32)
        mask = jnp.dot(repeat, mask, precision=HIGH, preferred_element_type=F32)
        weights[pl.ds(72 * x, 72), :] = by_atom * jnp.concatenate([mask, mask, mask], axis=0)

    tile = natural_tile(vec, above, below, 48)
    spread_columns(par[0] == 0, lambda slot, k: tile(slot - 2, k), range(2, 10), near, far, shift, 64)

    def emit(a, x, value):
        term[pl.ds((4 * a + x) * 64, 64), :] = value
        if x == 0:
            low_out[pl.ds(64 * a, 64), :] = value
        if x == 3:
            high_out[pl.ds(64 * a, 64), :] = value

    apply_operator(shift, weights, 64, emit)


def last_kernel(par, term, above, below, far, near, weights, vec, out, shift):
    spread_columns(par[0] == 0, blocked_tile(term, above, below), range(8), near, far, shift, 64)

    def emit(a, x, value):
        at = pl.ds(4 * a + x, 64, stride=12)
        out[at, :] = 2.0 * value - vec[at, :]

    apply_operator(shift, weights, 64, emit)


IN_SMEM = pl.BlockSpec(memory_space=pltpu.SMEM)
IN_VMEM = pl.BlockSpec(memory_space=pltpu.VMEM)
ANYWHERE = pl.BlockSpec(memory_space=pl.ANY)


def call(kernel, name, ins, outs, scratch=()):
    return pl.pallas_call(
        kernel,
        name=name,
        in_specs=ins,
        out_specs=[IN_VMEM] * len(outs),
        out_shape=[jax.ShapeDtypeStruct((rows, 128), F32) for rows in outs],
        scratch_shapes=[pltpu.VMEM((rows, 128), F32) if isinstance(rows, int) else rows for rows in scratch],
        compiler_params=pltpu.CompilerParams(vmem_limit_bytes=40 << 20),
    )


def along(value, axis, step):
    n = lax.axis_size(axis)
    return lax.ppermute(value, axis, [(i, (i + step) % n) for i in range(n)])


def from_both(columns):
    n = lax.axis_size("gy")
    near = lax.ppermute(columns, "gy", [(i, i ^ 1) for i in range(n)])
    pairs = [(i, (i + 1) % n) for i in range(1, n, 2)]
    far = lax.ppermute(columns, "gy", pairs + [(j, i) for i, j in pairs])
    return near, far


def shards(displacements, forces, neighbours, species, block_of, precond, vectors):
    snap = lax.axis_size("snap")
    scale = 1.0 / (displacements.shape[0] * snap * AB)
    disp = displacements.reshape(-1, 128)
    load = forces.reshape(-1, 128)
    vec = vectors.reshape(-1, 128)
    nbr = neighbours.reshape(-1, 128)
    par = (lax.axis_index("gy") % 2).astype(jnp.int32).reshape(1)

    low, high = call(rows_kernel, "rows", [ANYWHERE] * 2, (240, 240), (pltpu.SemaphoreType.DMA((4,)),))(
        displacements.reshape(-1, 4, 128), vectors.reshape(-1, 4, 128)
    )
    above, below = along(high, "gx", 1), along(low, "gx", -1)
    (columns,) = call(columns_kernel, "columns", [IN_VMEM] * 4, (32,))(disp, vec, above, below)
    near, far = from_both(columns)
    (part,) = call(
        functools.partial(gram_kernel, snap),
        "gram",
        [IN_SMEM] + [IN_VMEM] * 9,
        (snap * PAYLOAD,),
        (54 * 16, 27 * 64, len(PAIRS) * 8),
    )(par, disp, load, nbr, species, block_of, above, below, far, near)
    part = lax.all_to_all(part, "snap", 0, 0, tiled=True)
    theta, weights, term, low, high = call(
        functools.partial(fit_kernel, snap, scale),
        "fit",
        [IN_SMEM] + [IN_VMEM] * 10,
        (NP, 288, 768, 192, 192),
        (54 * 64,),
    )(par, part, precond.reshape(NG * NP, NP), vec, nbr, species, block_of, above, below, far, near)
    above, below = along(high, "gx", 1), along(low, "gx", -1)
    (columns,) = call(term_columns_kernel, "term_columns", [IN_VMEM] * 3, (24,))(term, above, below)
    near, far = from_both(columns)
    (result,) = call(last_kernel, "last", [IN_SMEM] + [IN_VMEM] * 7, (768,), (54 * 64,))(
        par, term, above, below, far, near, weights, vec
    )

    constants = theta.reshape(NP, 8, 16)[:, :3, :NG].transpose(2, 0, 1)
    return (
        constants.reshape(precond.shape[0], precond.shape[1], NP, 3),
        result.reshape(vectors.shape),
    )


def solution(mesh):
    in_specs = (
        P("snap", None, "gx", "gy"),
        P("snap", None, "gx", "gy"),
        P(None, "gx", "gy"),
        P("gx", "gy"),
        P("gx", "gy"),
        P(("gx", "gy"), None, None, None),
        P("snap", None, "gx", "gy"),
    )
    out_specs = (P(("gx", "gy"), None, None, None), P("snap", None, "gx", "gy"))
    return jax.shard_map(shards, mesh=mesh, in_specs=in_specs, out_specs=out_specs, check_vma=False)
```

```python
import functools

import jax
import jax.numpy as jnp
from jax import lax
from jax.experimental import pallas as pl
from jax.experimental.pallas import tpu as pltpu
from jax.sharding import PartitionSpec as P

AB = 128
NSPEC = 3
OFFSETS = ((-1, -1), (-1, 0), (-1, 1), (0, -1), (0, 1), (1, -1), (1, 0), (1, 1))
NG = 12
NP = 24
HIGH = lax.Precision.HIGHEST
F32 = jnp.float32


def lanes_of(shape):
    return lax.broadcasted_iota(jnp.int32, shape, 1)


def subs_of(shape):
    return lax.broadcasted_iota(jnp.int32, shape, 0)


def lane_slot(slot, k):
    return slot // 3, (slot % 3) * 36 + 2 * k


def pack_columns(tile_at, slots, columns):
    pair = lanes_of((8, 128)) // 2
    packed = [jnp.zeros((8, 128), F32) for _ in range(columns.shape[0] // 8)]
    for slot in slots:
        for k in range(18):
            t, at = lane_slot(slot, k)
            packed[t] = jnp.where(pair == at // 2, pltpu.roll(tile_at(slot, k), (at + 1) % 128, 1), packed[t])
    for t, value in enumerate(packed):
        columns[pl.ds(8 * t, 8), :] = value


def edge_tiles(even, slots, far_ref, near_ref):
    lane = lanes_of((8, 128))
    edges = {}
    for t in sorted({lane_slot(slot, 0)[0] for slot in slots}):
        near, far = near_ref[pl.ds(8 * t, 8), :], far_ref[pl.ds(8 * t, 8), :]
        left, right = jnp.where(even, far, near), jnp.where(even, near, far)
        edges[t] = jnp.where((lane & 1) == 0, pltpu.roll(right, 127, 1), pltpu.roll(left, 1, 1))

    def edge(slot, k):
        t, at = lane_slot(slot, k)
        return pltpu.roll(edges[t], 127 - at, 1)

    return edge


def spread_columns(edge, tile_at, slots, shift_ref, height):
    lane = lanes_of((8, 128))
    for k in range(18):
        for place, slot in enumerate(slots):
            values = tile_at(slot, k)
            outside = edge(slot, k)
            base = k * height + 8 * place
            shift_ref[pl.ds(base, 8), :] = jnp.where(lane == 0, outside, pltpu.roll(values, 1, 1))
            shift_ref[pl.ds(18 * height + base, 8), :] = values
            shift_ref[pl.ds(36 * height + base, 8), :] = jnp.where(lane == 127, outside, pltpu.roll(values, 127, 1))


def load_kernel(
    disp_in, vec_in, load_in, nbr_in, species, block_of, precond_in,
    disp, vec, low, high, load, nbr, group, precond, kind, block, sems,
):
    pairs = [(disp_in, disp), (vec_in, vec), (species, kind), (block_of, block), (load_in, load), (nbr_in, nbr)]
    pairs.append((precond_in, precond))
    copies = [pltpu.make_async_copy(source, out, sems.at[i]) for i, (source, out) in enumerate(pairs)]
    for copy in copies:
        copy.start()
    copies[0].wait()
    copies[1].wait()
    for out, x in ((low, 0), (high, 3)):
        out[pl.ds(0, 48), :] = disp[pl.ds(x, 48, stride=4), :]
        out[pl.ds(48, 192), :] = vec[pl.ds(x, 192, stride=4), :]
    for copy in copies[2:]:
        copy.wait()
    group[...] = block[...] * NSPEC + kind[...]


def natural_tile(source, above, below, base):
    def tile(place, k):
        b, x = k // 6, k % 6 - 1
        if 0 <= x < 4:
            return source[pl.ds(12 * 8 * place + 4 * b + x, 8, stride=12), :]
        return (above if x < 0 else below)[pl.ds(base + 24 * place + b, 8, stride=3), :]

    return tile


def term_tile(low, mid, high, above, below):
    def tile(place, k):
        b, x = k // 6, k % 6 - 1
        if x in (1, 2):
            return mid[pl.ds((2 * b + x - 1) * 64 + 8 * place, 8), :]
        return {-1: above, 0: low, 3: high, 4: below}[x][pl.ds(b * 64 + 8 * place, 8), :]

    return tile


def columns_kernel(disp, vec, above, below, columns):
    disp_tile = natural_tile(disp, above, below, 0)
    vec_tile = natural_tile(vec, above, below, 48)
    pack_columns(lambda slot, k: disp_tile(slot, k) if slot < 2 else vec_tile(slot - 2, k), range(10), columns)


def term_columns_kernel(low, mid, high, above, below, columns):
    pack_columns(term_tile(low, mid, high, above, below), range(8), columns)


def fold_rows(tiles, sub):
    for bit in (1, 2, 4):
        low = (sub & bit) == 0
        tiles = [
            jnp.where(low, tiles[2 * i], tiles[2 * i + 1])
            + pltpu.roll(jnp.where(low, tiles[2 * i + 1], tiles[2 * i]), bit, 0)
            for i in range(len(tiles) // 2)
        ]
    return tiles[0]


def fold_lanes(tiles, eighth):
    for bit in (1, 2, 4):
        low = (eighth & bit) == 0
        tiles = [
            jnp.where(low, tiles[2 * i], tiles[2 * i + 1])
            + pltpu.roll(jnp.where(low, tiles[2 * i + 1], tiles[2 * i]), 16 * bit, 1)
            for i in range(len(tiles) // 2)
        ]
    return tiles[0]


PAIRS = [(q, p) for q in range(NP) for p in range(q, NP + 3)]
PAIR_AT = {pair: i for i, pair in enumerate(PAIRS)}
BLOCKS = [(i, j) for i in range(3) for j in range(i, 3)]
PAYLOAD = 64
CHUNK = 62


def gram_kernel(copies, par, disp, forces, nbr, group, above, below, near, far, out, shift, feats, sums):
    edge = edge_tiles(par[0] == 0, range(2), far, near)
    spread_columns(edge, natural_tile(disp, above, below, 0), range(2), shift, 16)
    for x in range(4):
        for o, (dx, dy) in enumerate(OFFSETS):
            mask = nbr[pl.ds(4 * o + x, 1), :].astype(F32)
            for b in range(3):
                moved = shift[pl.ds(((dy + 1) * 18 + 6 * b + x + dx + 1) * 16, 16), :]
                center = shift[pl.ds((18 + 6 * b + x + 1) * 16, 16), :]
                feats[pl.ds((3 * o + b) * 64 + x, 16, stride=4), :] = (moved - center) * mask
        for a in range(3):
            feats[pl.ds((NP + a) * 64 + x, 16, stride=4), :] = forces[pl.ds(4 * a + x, 16, stride=12), :]
    for q in range(NP):
        left = feats[pl.ds(q * 64, 64), :].reshape(8, 8, 128)
        for p in range(q, NP + 3):
            right = feats[pl.ds(p * 64, 64), :].reshape(8, 8, 128)
            sums[pl.ds(PAIR_AT[q, p] * 8, 8), :] = jnp.sum(left * right, axis=0)
    which = subs_of((16, 128))
    members = jnp.concatenate([(which == group[pl.ds(x % 4, 1), :]).astype(F32) for x in range(8)], axis=0)
    members = members.astype(jnp.bfloat16)
    members = jnp.concatenate([members, members], axis=1)
    sub, eighth = subs_of((8, 128)), lanes_of((8, 128)) // 16
    own = (sub == eighth).astype(F32)
    for c in range(len(PAIRS) // CHUNK):
        at = pl.ds(c * CHUNK * 8, CHUNK * 8)
        value = sums[at, :]
        high = value.astype(jnp.bfloat16)
        low = (value - high.astype(F32)).astype(jnp.bfloat16)
        by_group = lax.dot_general(
            jnp.concatenate([high, low], axis=1), members, (((1,), (1,)), ((), ())), preferred_element_type=F32
        )
        sums[at, :] = (by_group.reshape(CHUNK, 8, 128) * own[None]).reshape(CHUNK * 8, 128)

    def column(fixed, block):
        pairs = [(min(fixed, 8 * block + r), max(fixed, 8 * block + r)) for r in range(8)]
        return fold_rows([sums[pl.ds(PAIR_AT[pair] * 8, 8), :] for pair in pairs], sub)

    packed = [fold_lanes([column(8 * i + r, j) for r in range(8)], eighth) for i, j in BLOCKS]
    sides = [column(NP + a, block) for a in range(3) for block in range(3)] + [jnp.zeros((8, 128), F32)] * 7
    packed += [fold_lanes(sides[:8], eighth), fold_lanes(sides[8:], eighth)]
    for i, value in enumerate(packed):
        for copy in range(copies):
            out[pl.ds(copy * PAYLOAD + 8 * i, 8), :] = value


def apply_operator(shift, weights, lattice_rows, emit):
    for x in lattice_rows:
        total = [None] * 3
        for b in range(3):
            center = shift[pl.ds((18 + 6 * b + x + 1) * 64, 64), :]
            for o, (dx, dy) in enumerate(OFFSETS):
                moved = shift[pl.ds(((dy + 1) * 18 + 6 * b + x + dx + 1) * 64, 64), :]
                differ = center - moved
                for a in range(3):
                    term = differ * weights[pl.ds(72 * x + 24 * a + 3 * o + b, 1), :]
                    total[a] = term if total[a] is None else total[a] + term
        for a in range(3):
            emit(a, x, total[a])


def fit_kernel(
    copies, scale, par, sums, precond, vec, nbr, group, above, below, near, far,
    theta, weights, low_out, high_out, shift,
):
    sub, eighth = subs_of((8, 128)), lanes_of((8, 128)) // 16

    def total(i):
        value = sums[pl.ds(8 * i, 8), :]
        for copy in range(1, copies):
            value = value + sums[pl.ds(copy * PAYLOAD + 8 * i, 8), :]
        return value * scale

    def spread(value, k):
        value = jnp.where(eighth == k, value, 0.0)
        for step in (16, 32, 64):
            value = value + pltpu.roll(value, step, 1)
        return value

    sides = [spread(total(6 + i // 8), i % 8) for i in range(9)]
    rhs = []
    for block in range(3):
        value = jnp.where(eighth == 0, sides[block], 0.0)
        for a in (1, 2):
            value = jnp.where(eighth == a, sides[3 * a + block], value)
        rhs.append(value)
    of_group = lanes_of((NP, 128)) & 15

    def solve(right):
        every = jnp.dot(precond[...], right, precision=HIGH, preferred_element_type=F32)
        result = every[0:NP]
        for g in range(1, NG):
            result = jnp.where(of_group == g, every[g * NP : (g + 1) * NP], result)
        return result

    first = solve(jnp.concatenate(rhs, axis=0))
    part = [first[8 * i : 8 * i + 8] for i in range(3)]
    remain = list(rhs)
    for m, (i, j) in enumerate(BLOCKS):
        value = total(m)
        tiles = [spread(value, r) for r in range(8)]
        for r in range(8):
            remain[j] = remain[j] - tiles[r] * part[i][r : r + 1, :]
        if i != j:
            remain[i] = remain[i] - fold_rows([tiles[r] * part[j] for r in range(8)], sub)
    fitted = first + solve(jnp.concatenate(remain, axis=0))
    theta[...] = fitted

    of_part = lanes_of((NP, 128)) // 16
    stacked = jnp.concatenate(
        [jnp.where((of_part == a) & (of_group < NG), fitted, 0.0) for a in range(3)], axis=0
    )
    which = subs_of((128, 128)) & 15
    p_row, o_col = subs_of((NP, 8)), lanes_of((NP, 8))
    repeat = ((p_row >= 3 * o_col) & (p_row < 3 * o_col + 3)).astype(F32)
    for x in range(4):
        member = (which == group[pl.ds(x, 1), :]).astype(F32)
        by_atom = jnp.dot(stacked, member, precision=HIGH, preferred_element_type=F32)
        mask = nbr[pl.ds(x, 8, stride=4), :].astype(F32)
        mask = jnp.dot(repeat, mask, precision=HIGH, preferred_element_type=F32)
        weights[pl.ds(72 * x, 72), :] = by_atom * jnp.concatenate([mask, mask, mask], axis=0)

    tile = natural_tile(vec, above, below, 48)
    edge = edge_tiles(par[0] == 0, range(2, 10), far, near)
    spread_columns(edge, lambda slot, k: tile(slot - 2, k), range(2, 10), shift, 64)

    def emit(a, x, value):
        (high_out if x else low_out)[pl.ds(64 * a, 64), :] = value

    apply_operator(shift, weights, (0, 3), emit)


def middle_kernel(shift, weights, theta, mid, constants):
    def emit(a, x, value):
        mid[pl.ds((2 * a + x - 1) * 64, 64), :] = value

    apply_operator(shift, weights, (1, 2), emit)
    row, lane = subs_of((36, 128)), lanes_of((36, 128))
    which = row >> 2
    kind = (which >= 3).astype(jnp.int32) + (which >= 6).astype(jnp.int32)
    pick = (lane == 16 * (which - 3 * kind) + 3 * (row & 3) + kind).astype(F32)
    constants[...] = lax.dot_general(
        pick, theta[...], (((1,), (1,)), ((), ())), precision=HIGH, preferred_element_type=F32
    )


def inner_kernel(low, mid, high, above, below, weights, vec, out, shift):
    empty = jnp.zeros((8, 128), F32)
    spread_columns(lambda slot, k: empty, term_tile(low, mid, high, above, below), range(8), shift, 64)

    def emit(a, x, value):
        out[pl.ds((4 * a + x) * 64, 64), :] = 2.0 * value - vec[pl.ds(4 * a + x, 64, stride=12), :]

    apply_operator(shift, weights, range(4), emit)


def outer_kernel(par, inner, near, far, weights, out, edges):
    edge = edge_tiles(par[0] == 0, range(8), far, near)
    for k in range(18):
        for slot in range(8):
            edges[pl.ds(64 * k + 8 * slot, 8), :] = edge(slot, k)
    lane = lanes_of((1, 128))
    for x in range(4):
        total = [inner[pl.ds((4 * a + x) * 64, 64), :] for a in range(3)]
        for b in range(3):
            for dx in (-1, 0, 1):
                outside = edges[pl.ds(64 * (6 * b + x + dx + 1), 64), :]
                for a in range(3):
                    base = 72 * x + 24 * a + b
                    left = weights[pl.ds(base + 3 * OFFSETS.index((dx, -1)), 1), :]
                    right = weights[pl.ds(base + 3 * OFFSETS.index((dx, 1)), 1), :]
                    weight = jnp.where(lane == 0, 2.0 * left, jnp.where(lane == 127, 2.0 * right, 0.0))
                    total[a] = total[a] - outside * weight
        for a in range(3):
            out[pl.ds(4 * a + x, 64, stride=12), :] = total[a]


IN_SMEM = pl.BlockSpec(memory_space=pltpu.SMEM)
IN_VMEM = pl.BlockSpec(memory_space=pltpu.VMEM)
IN_HBM = pl.BlockSpec(memory_space=pltpu.HBM)


def call(kernel, name, ins, outs, scratch=(), flops=0):
    outs = [jax.ShapeDtypeStruct((rows, 128), F32) if isinstance(rows, int) else rows for rows in outs]
    return pl.pallas_call(
        kernel,
        name=name,
        in_specs=ins,
        out_specs=[IN_VMEM] * len(outs),
        out_shape=outs,
        scratch_shapes=[pltpu.VMEM((rows, 128), F32) if isinstance(rows, int) else rows for rows in scratch],
        compiler_params=pltpu.CompilerParams(vmem_limit_bytes=40 << 20),
        cost_estimate=pl.CostEstimate(flops=flops, bytes_accessed=1 << 20, transcendentals=0),
    )


def along(value, axis, step):
    n = lax.axis_size(axis)
    return lax.ppermute(value, axis, [(i, (i + step) % n) for i in range(n)])


def from_both(columns):
    n = lax.axis_size("gy")
    near = lax.ppermute(columns, "gy", [(i, i ^ 1) for i in range(n)])
    pairs = [(i, (i + 1) % n) for i in range(1, n, 2)]
    far = lax.ppermute(columns, "gy", pairs + [(j, i) for i, j in pairs])
    return near, far


def shards(displacements, forces, neighbours, species, block_of, precond, vectors):
    snap = lax.axis_size("snap")
    scale = 1.0 / (displacements.shape[0] * snap * AB)
    par = (lax.axis_index("gy") % 2).astype(jnp.int32).reshape(1)

    whole = [
        pltpu.with_memory_space_constraint(value, pltpu.HBM)
        for value in (
            displacements.reshape(-1, 128),
            vectors.reshape(-1, 128),
            forces.reshape(-1, 128),
            neighbours.reshape(-1, 128),
            species,
            block_of,
            precond.reshape(NG * NP, NP),
        )
    ]
    tile = jax.ShapeDtypeStruct((4, 128), jnp.int32)
    disp, vec, low, high, load, nbr, group, inverses = call(
        load_kernel,
        "load",
        [IN_HBM] * 7,
        (192, 768, 240, 240, 192, jax.ShapeDtypeStruct((32, 128), jnp.int32), tile, jax.ShapeDtypeStruct((NG * NP, NP), F32)),
        (pltpu.VMEM((4, 128), jnp.int32), pltpu.VMEM((4, 128), jnp.int32), pltpu.SemaphoreType.DMA((7,))),
    )(*whole)
    above, below = along(high, "gx", 1), along(low, "gx", -1)
    (columns,) = call(columns_kernel, "columns", [IN_VMEM] * 4, (32,))(disp, vec, above, below)
    near, far = from_both(columns)
    (part,) = call(
        functools.partial(gram_kernel, snap),
        "gram",
        [IN_SMEM] + [IN_VMEM] * 8,
        (snap * PAYLOAD,),
        (54 * 16, 27 * 64, len(PAIRS) * 8),
    )(par, disp, load, nbr, group, above, below, near, far)
    part = lax.all_to_all(part, "snap", 0, 0, tiled=True)
    theta, weights, low, high, shift = call(
        functools.partial(fit_kernel, snap, scale),
        "fit",
        [IN_SMEM] + [IN_VMEM] * 9,
        (NP, 288, 192, 192, 54 * 64),
    )(par, part, inverses, vec, nbr, group, above, below, near, far)
    above, below = along(high, "gx", 1), along(low, "gx", -1)
    mid, constants = call(
        middle_kernel,
        "middle",
        [IN_VMEM] * 3,
        (384, jax.ShapeDtypeStruct((3 * NG, NP), F32)),
        flops=1 << 24,
    )(shift, weights, theta)
    (columns,) = call(term_columns_kernel, "term_columns", [IN_VMEM] * 5, (24,))(low, mid, high, above, below)
    near, far = from_both(columns)
    (inner,) = call(inner_kernel, "inner", [IN_VMEM] * 7, (768,), (54 * 64,), flops=1 << 25)(
        low, mid, high, above, below, weights, vec
    )
    (result,) = call(outer_kernel, "outer", [IN_SMEM] + [IN_VMEM] * 4, (768,), (18 * 64,))(
        par, inner, near, far, weights
    )

    constants = constants.reshape(NSPEC, 3, precond.shape[0], NP).transpose(2, 0, 3, 1)
    return (constants, result.reshape(vectors.shape))


def solution(mesh):
    in_specs = (
        P("snap", None, "gx", "gy"),
        P("snap", None, "gx", "gy"),
        P(None, "gx", "gy"),
        P("gx", "gy"),
        P("gx", "gy"),
        P(("gx", "gy"), None, None, None),
        P("snap", None, "gx", "gy"),
    )
    out_specs = (P(("gx", "gy"), None, None, None), P("snap", None, "gx", "gy"))
    return jax.shard_map(shards, mesh=mesh, in_specs=in_specs, out_specs=out_specs, check_vma=False)
```

```python
import functools

import jax
import jax.numpy as jnp
from jax import lax
from jax.experimental import pallas as pl
from jax.experimental.pallas import tpu as pltpu
from jax.sharding import PartitionSpec as P

AB = 128
NSPEC = 3
OFFSETS = ((-1, -1), (-1, 0), (-1, 1), (0, -1), (0, 1), (1, -1), (1, 0), (1, 1))
NG = 12
NP = 24
HIGH = lax.Precision.HIGHEST
F32 = jnp.float32


def lanes_of(shape):
    return lax.broadcasted_iota(jnp.int32, shape, 1)


def subs_of(shape):
    return lax.broadcasted_iota(jnp.int32, shape, 0)


def lane_slot(slot, k):
    return slot // 3, (slot % 3) * 36 + 2 * k


def pack_columns(tile_at, slots, columns):
    pair = lanes_of((8, 128)) // 2
    packed = [jnp.zeros((8, 128), F32) for _ in range(columns.shape[0] // 8)]
    for slot in slots:
        for k in range(18):
            t, at = lane_slot(slot, k)
            packed[t] = jnp.where(pair == at // 2, pltpu.roll(tile_at(slot, k), (at + 1) % 128, 1), packed[t])
    for t, value in enumerate(packed):
        columns[pl.ds(8 * t, 8), :] = value


def edge_tiles(even, slots, far_ref, near_ref):
    lane = lanes_of((8, 128))
    edges = {}
    for t in sorted({lane_slot(slot, 0)[0] for slot in slots}):
        near, far = near_ref[pl.ds(8 * t, 8), :], far_ref[pl.ds(8 * t, 8), :]
        left, right = jnp.where(even, far, near), jnp.where(even, near, far)
        edges[t] = jnp.where((lane & 1) == 0, pltpu.roll(right, 127, 1), pltpu.roll(left, 1, 1))

    def edge(slot, k):
        t, at = lane_slot(slot, k)
        return pltpu.roll(edges[t], 127 - at, 1)

    return edge


def spread_columns(edge, tile_at, slots, shift_ref, height):
    lane = lanes_of((8, 128))
    for k in range(18):
        for place, slot in enumerate(slots):
            values = tile_at(slot, k)
            outside = edge(slot, k)
            base = k * height + 8 * place
            shift_ref[pl.ds(base, 8), :] = jnp.where(lane == 0, outside, pltpu.roll(values, 1, 1))
            shift_ref[pl.ds(18 * height + base, 8), :] = values
            shift_ref[pl.ds(36 * height + base, 8), :] = jnp.where(lane == 127, outside, pltpu.roll(values, 127, 1))


def rows_kernel(disp, vec, low, high, sems):
    copies = []
    for out, x in ((low, 0), (high, 3)):
        for source, at in ((disp, pl.ds(0, 48)), (vec, pl.ds(48, 192))):
            copies.append(pltpu.make_async_copy(source.at[:, x, :], out.at[at, :], sems.at[len(copies)]))
    for copy in copies:
        copy.start()
    for copy in copies:
        copy.wait()


def load_kernel(
    disp_in, vec_in, load_in, nbr_in, species, block_of, precond_in,
    disp, vec, load, nbr, group, precond, masks, members, kind, block, sems,
):
    pairs = [(disp_in, disp), (vec_in, vec), (species, kind), (block_of, block), (load_in, load), (nbr_in, nbr)]
    pairs.append((precond_in, precond))
    copies = [pltpu.make_async_copy(source, out, sems.at[i]) for i, (source, out) in enumerate(pairs)]
    for copy in copies:
        copy.start()
    for copy in copies:
        copy.wait()
    group[...] = block[...] * NSPEC + kind[...]
    which = subs_of((128, 128)) & 15
    p_row, o_col = subs_of((NP, 8)), lanes_of((NP, 8))
    repeat = ((p_row >= 3 * o_col) & (p_row < 3 * o_col + 3)).astype(jnp.bfloat16)
    for x in range(4):
        mask = nbr[pl.ds(x, 8, stride=4), :].astype(F32).astype(jnp.bfloat16)
        masks[pl.ds(NP * x, NP), :] = jnp.dot(repeat, mask, preferred_element_type=F32)
        members[:, pl.ds(128 * x, 128)] = (which == group[pl.ds(x, 1), :]).astype(F32).astype(jnp.bfloat16)


def natural_tile(source, above, below, base):
    def tile(place, k):
        b, x = k // 6, k % 6 - 1
        if 0 <= x < 4:
            return source[pl.ds(12 * 8 * place + 4 * b + x, 8, stride=12), :]
        return (above if x < 0 else below)[pl.ds(base + 24 * place + b, 8, stride=3), :]

    return tile


def term_tile(low, mid, high, above, below):
    def tile(place, k):
        b, x = k // 6, k % 6 - 1
        if x in (1, 2):
            return mid[pl.ds((2 * b + x - 1) * 64 + 8 * place, 8), :]
        return {-1: above, 0: low, 3: high, 4: below}[x][pl.ds(b * 64 + 8 * place, 8), :]

    return tile


def columns_kernel(disp, vec, above, below, columns):
    disp_tile = natural_tile(disp, above, below, 0)
    vec_tile = natural_tile(vec, above, below, 48)
    pack_columns(lambda slot, k: disp_tile(slot, k) if slot < 2 else vec_tile(slot - 2, k), range(10), columns)


def term_columns_kernel(low, mid, high, above, below, columns):
    pack_columns(term_tile(low, mid, high, above, below), range(8), columns)


def fold_rows(tiles, sub):
    for bit in (1, 2, 4):
        low = (sub & bit) == 0
        tiles = [
            jnp.where(low, tiles[2 * i], tiles[2 * i + 1])
            + pltpu.roll(jnp.where(low, tiles[2 * i + 1], tiles[2 * i]), bit, 0)
            for i in range(len(tiles) // 2)
        ]
    return tiles[0]


def fold_lanes(tiles, eighth):
    for bit in (1, 2, 4):
        low = (eighth & bit) == 0
        tiles = [
            jnp.where(low, tiles[2 * i], tiles[2 * i + 1])
            + pltpu.roll(jnp.where(low, tiles[2 * i + 1], tiles[2 * i]), 16 * bit, 1)
            for i in range(len(tiles) // 2)
        ]
    return tiles[0]


PAIRS = [(q, p) for q in range(NP) for p in range(q, NP + 3)]
PAIR_AT = {pair: i for i, pair in enumerate(PAIRS)}
BLOCKS = [(i, j) for i in range(3) for j in range(i, 3)]
PAYLOAD = 64
CHUNK = 62


def gram_kernel(copies, par, disp, forces, nbr, group, above, below, near, far, out, shift, feats, sums):
    edge = edge_tiles(par[0] == 0, range(2), far, near)
    spread_columns(edge, natural_tile(disp, above, below, 0), range(2), shift, 16)
    for x in range(4):
        for o, (dx, dy) in enumerate(OFFSETS):
            mask = nbr[pl.ds(4 * o + x, 1), :].astype(F32)
            for b in range(3):
                moved = shift[pl.ds(((dy + 1) * 18 + 6 * b + x + dx + 1) * 16, 16), :]
                center = shift[pl.ds((18 + 6 * b + x + 1) * 16, 16), :]
                feats[pl.ds((3 * o + b) * 64 + x, 16, stride=4), :] = (moved - center) * mask
        for a in range(3):
            feats[pl.ds((NP + a) * 64 + x, 16, stride=4), :] = forces[pl.ds(4 * a + x, 16, stride=12), :]
    for q in range(NP):
        left = feats[pl.ds(q * 64, 64), :].reshape(8, 8, 128)
        for p in range(q, NP + 3):
            right = feats[pl.ds(p * 64, 64), :].reshape(8, 8, 128)
            sums[pl.ds(PAIR_AT[q, p] * 8, 8), :] = jnp.sum(left * right, axis=0)
    which = subs_of((16, 128))
    members = jnp.concatenate([(which == group[pl.ds(x % 4, 1), :]).astype(F32) for x in range(8)], axis=0)
    members = members.astype(jnp.bfloat16)
    members = jnp.concatenate([members, members], axis=1)
    sub, eighth = subs_of((8, 128)), lanes_of((8, 128)) // 16
    own = (sub == eighth).astype(F32)
    for c in range(len(PAIRS) // CHUNK):
        at = pl.ds(c * CHUNK * 8, CHUNK * 8)
        value = sums[at, :]
        high = value.astype(jnp.bfloat16)
        low = (value - high.astype(F32)).astype(jnp.bfloat16)
        by_group = lax.dot_general(
            jnp.concatenate([high, low], axis=1), members, (((1,), (1,)), ((), ())), preferred_element_type=F32
        )
        sums[at, :] = (by_group.reshape(CHUNK, 8, 128) * own[None]).reshape(CHUNK * 8, 128)

    def column(fixed, block):
        pairs = [(min(fixed, 8 * block + r), max(fixed, 8 * block + r)) for r in range(8)]
        return fold_rows([sums[pl.ds(PAIR_AT[pair] * 8, 8), :] for pair in pairs], sub)

    packed = [fold_lanes([column(8 * i + r, j) for r in range(8)], eighth) for i, j in BLOCKS]
    sides = [column(NP + a, block) for a in range(3) for block in range(3)] + [jnp.zeros((8, 128), F32)] * 7
    packed += [fold_lanes(sides[:8], eighth), fold_lanes(sides[8:], eighth)]
    for i, value in enumerate(packed):
        for copy in range(copies):
            out[pl.ds(copy * PAYLOAD + 8 * i, 8), :] = value


def apply_operator(shift, weights, lattice_rows, emit):
    for x in lattice_rows:
        total = [None] * 3
        for b in range(3):
            center = shift[pl.ds((18 + 6 * b + x + 1) * 64, 64), :]
            for o, (dx, dy) in enumerate(OFFSETS):
                moved = shift[pl.ds(((dy + 1) * 18 + 6 * b + x + dx + 1) * 64, 64), :]
                differ = center - moved
                for a in range(3):
                    term = differ * weights[pl.ds(72 * x + 24 * a + 3 * o + b, 1), :]
                    total[a] = term if total[a] is None else total[a] + term
        for a in range(3):
            emit(a, x, total[a])


def fit_kernel(
    copies, scale, par, sums, precond, vec, masks, members, above, below, near, far,
    theta, weights, low_out, high_out, shift,
):
    sub, eighth = subs_of((8, 128)), lanes_of((8, 128)) // 16

    def total(i):
        value = sums[pl.ds(8 * i, 8), :]
        for copy in range(1, copies):
            value = value + sums[pl.ds(copy * PAYLOAD + 8 * i, 8), :]
        return value * scale

    def spread(value, k):
        value = jnp.where(eighth == k, value, 0.0)
        for step in (16, 32, 64):
            value = value + pltpu.roll(value, step, 1)
        return value

    sides = [spread(total(6 + i // 8), i % 8) for i in range(9)]
    rhs = []
    for block in range(3):
        value = jnp.where(eighth == 0, sides[block], 0.0)
        for a in (1, 2):
            value = jnp.where(eighth == a, sides[3 * a + block], value)
        rhs.append(value)
    of_group = lanes_of((NP, 128)) & 15

    def solve(right):
        every = jnp.dot(precond[...], right, precision=HIGH, preferred_element_type=F32)
        result = every[0:NP]
        for g in range(1, NG):
            result = jnp.where(of_group == g, every[g * NP : (g + 1) * NP], result)
        return result

    first = solve(jnp.concatenate(rhs, axis=0))
    part = [first[8 * i : 8 * i + 8] for i in range(3)]
    remain = list(rhs)
    for m, (i, j) in enumerate(BLOCKS):
        value = total(m)
        tiles = [spread(value, r) for r in range(8)]
        for r in range(8):
            remain[j] = remain[j] - tiles[r] * part[i][r : r + 1, :]
        if i != j:
            remain[i] = remain[i] - fold_rows([tiles[r] * part[j] for r in range(8)], sub)
    fitted = first + solve(jnp.concatenate(remain, axis=0))
    theta[...] = fitted

    of_part = lanes_of((NP, 128)) // 16
    stacked = jnp.concatenate(
        [jnp.where((of_part == a) & (of_group < NG), fitted, 0.0) for a in range(3)], axis=0
    )
    by_atom = None
    for _ in range(3):
        piece = stacked.astype(jnp.bfloat16)
        stacked = stacked - piece.astype(F32)
        term = jnp.dot(piece, members[...], preferred_element_type=F32)
        by_atom = term if by_atom is None else by_atom + term
    for x in range(4):
        mask = masks[pl.ds(NP * x, NP), :]
        weights[pl.ds(72 * x, 72), :] = by_atom[:, 128 * x : 128 * x + 128] * jnp.concatenate([mask] * 3, axis=0)

    tile = natural_tile(vec, above, below, 48)
    edge = edge_tiles(par[0] == 0, range(2, 10), far, near)
    spread_columns(edge, lambda slot, k: tile(slot - 2, k), range(2, 10), shift, 64)

    def emit(a, x, value):
        (high_out if x else low_out)[pl.ds(64 * a, 64), :] = value

    apply_operator(shift, weights, (0, 3), emit)


def middle_kernel(shift, weights, theta, mid, constants):
    def emit(a, x, value):
        mid[pl.ds((2 * a + x - 1) * 64, 64), :] = value

    apply_operator(shift, weights, (1, 2), emit)
    row, lane = subs_of((36, 128)), lanes_of((36, 128))
    which = row >> 2
    kind = (which >= 3).astype(jnp.int32) + (which >= 6).astype(jnp.int32)
    pick = (lane == 16 * (which - 3 * kind) + 3 * (row & 3) + kind).astype(F32)
    picked = lax.dot_general(
        pick, theta[...], (((1,), (1,)), ((), ())), precision=HIGH, preferred_element_type=F32
    )
    for i in range(9):
        constants[i] = picked[4 * i : 4 * i + 4]


def inner_kernel(low, mid, high, above, below, weights, vec, out, shift):
    empty = jnp.zeros((8, 128), F32)
    spread_columns(lambda slot, k: empty, term_tile(low, mid, high, above, below), range(8), shift, 64)

    def emit(a, x, value):
        out[pl.ds((4 * a + x) * 64, 64), :] = 2.0 * value - vec[pl.ds(4 * a + x, 64, stride=12), :]

    apply_operator(shift, weights, range(4), emit)


def outer_kernel(par, inner, near, far, weights, out, edges, result, sems):
    edge = edge_tiles(par[0] == 0, range(8), far, near)
    lane = lanes_of((1, 128))
    copies = []
    for half in range(2):
        for k in range(18):
            for slot in range(4 * half, 4 * half + 4):
                edges[pl.ds(64 * k + 8 * slot, 8), :] = edge(slot, k)
        for x in range(4):
            total = [inner[pl.ds((4 * a + x) * 64 + 32 * half, 32), :] for a in range(3)]
            for b in range(3):
                for dx in (-1, 0, 1):
                    outside = edges[pl.ds(64 * (6 * b + x + dx + 1) + 32 * half, 32), :]
                    for a in range(3):
                        base = 72 * x + 24 * a + b
                        left = weights[pl.ds(base + 3 * OFFSETS.index((dx, -1)), 1), :]
                        right = weights[pl.ds(base + 3 * OFFSETS.index((dx, 1)), 1), :]
                        weight = jnp.where(lane == 0, 2.0 * left, jnp.where(lane == 127, 2.0 * right, 0.0))
                        total[a] = total[a] - outside * weight
            for a in range(3):
                result[pl.ds(384 * half + 4 * a + x, 32, stride=12), :] = total[a]
        rows = pl.ds(384 * half, 384)
        copies.append(pltpu.make_async_copy(result.at[rows, :], out.at[rows, :], sems.at[half]))
        copies[half].start()
    for copy in copies:
        copy.wait()


IN_SMEM = pl.BlockSpec(memory_space=pltpu.SMEM)
IN_VMEM = pl.BlockSpec(memory_space=pltpu.VMEM)
IN_HBM = pl.BlockSpec(memory_space=pltpu.HBM)


def call(kernel, name, ins, outs, scratch=(), flops=0, out_spec=IN_VMEM):
    outs = [jax.ShapeDtypeStruct((rows, 128), F32) if isinstance(rows, int) else rows for rows in outs]
    return pl.pallas_call(
        kernel,
        name=name,
        in_specs=ins,
        out_specs=[out_spec] * len(outs),
        out_shape=outs,
        scratch_shapes=[pltpu.VMEM((rows, 128), F32) if isinstance(rows, int) else rows for rows in scratch],
        compiler_params=pltpu.CompilerParams(vmem_limit_bytes=40 << 20),
        cost_estimate=pl.CostEstimate(flops=flops, bytes_accessed=1 << 20, transcendentals=0),
    )


def along(value, axis, step):
    n = lax.axis_size(axis)
    return lax.ppermute(value, axis, [(i, (i + step) % n) for i in range(n)])


def from_both(columns):
    n = lax.axis_size("gy")
    near = lax.ppermute(columns, "gy", [(i, i ^ 1) for i in range(n)])
    pairs = [(i, (i + 1) % n) for i in range(1, n, 2)]
    far = lax.ppermute(columns, "gy", pairs + [(j, i) for i, j in pairs])
    return near, far


def shards(displacements, forces, neighbours, species, block_of, precond, vectors):
    snap = lax.axis_size("snap")
    scale = 1.0 / (displacements.shape[0] * snap * AB)
    par = (lax.axis_index("gy") % 2).astype(jnp.int32).reshape(1)

    def in_hbm(*values):
        return [pltpu.with_memory_space_constraint(value, pltpu.HBM) for value in values]

    low, high = call(rows_kernel, "rows", [IN_HBM] * 2, (240, 240), (pltpu.SemaphoreType.DMA((4,)),))(
        *in_hbm(displacements.reshape(-1, 4, 128), vectors.reshape(-1, 4, 128))
    )
    above, below = along(high, "gx", 1), along(low, "gx", -1)
    tile = jax.ShapeDtypeStruct((4, 128), jnp.int32)
    disp, vec, load, nbr, group, inverses, masks, members = call(
        load_kernel,
        "load",
        [IN_HBM] * 7,
        (
            192,
            768,
            192,
            jax.ShapeDtypeStruct((32, 128), jnp.int32),
            tile,
            jax.ShapeDtypeStruct((NG * NP, NP), F32),
            4 * NP,
            jax.ShapeDtypeStruct((128, 512), jnp.bfloat16),
        ),
        (pltpu.VMEM((4, 128), jnp.int32), pltpu.VMEM((4, 128), jnp.int32), pltpu.SemaphoreType.DMA((7,))),
        flops=1 << 24,
    )(
        *in_hbm(
            displacements.reshape(-1, 128),
            vectors.reshape(-1, 128),
            forces.reshape(-1, 128),
            neighbours.reshape(-1, 128),
            species,
            block_of,
            precond.reshape(NG * NP, NP),
        )
    )
    (columns,) = call(columns_kernel, "columns", [IN_VMEM] * 4, (32,))(disp, vec, above, below)
    near, far = from_both(columns)
    (part,) = call(
        functools.partial(gram_kernel, snap),
        "gram",
        [IN_SMEM] + [IN_VMEM] * 8,
        (snap * PAYLOAD,),
        (54 * 16, 27 * 64, len(PAIRS) * 8),
    )(par, disp, load, nbr, group, above, below, near, far)
    part = lax.all_to_all(part, "snap", 0, 0, tiled=True)
    theta, weights, low, high, shift = call(
        functools.partial(fit_kernel, snap, scale),
        "fit",
        [IN_SMEM] + [IN_VMEM] * 9,
        (NP, 288, 192, 192, 54 * 64),
    )(par, part, inverses, vec, masks, members, above, below, near, far)
    above, below = along(high, "gx", 1), along(low, "gx", -1)
    mid, constants = call(
        middle_kernel,
        "middle",
        [IN_VMEM] * 3,
        (384, jax.ShapeDtypeStruct((9, 4, NP), F32)),
        flops=1 << 24,
    )(shift, weights, theta)
    (columns,) = call(term_columns_kernel, "term_columns", [IN_VMEM] * 5, (24,))(low, mid, high, above, below)
    near, far = from_both(columns)
    (inner,) = call(inner_kernel, "inner", [IN_VMEM] * 7, (768,), (54 * 64,), flops=1 << 25)(
        low, mid, high, above, below, weights, vec
    )
    (result,) = call(
        outer_kernel,
        "outer",
        [IN_SMEM] + [IN_VMEM] * 4,
        (768,),
        (18 * 64, 768, pltpu.SemaphoreType.DMA((2,))),
        out_spec=IN_HBM,
    )(
        par, inner, near, far, weights
    )

    constants = constants.reshape(NSPEC, 3, precond.shape[0], NP).transpose(2, 0, 3, 1)
    return (constants, result.reshape(vectors.shape))


def solution(mesh):
    in_specs = (
        P("snap", None, "gx", "gy"),
        P("snap", None, "gx", "gy"),
        P(None, "gx", "gy"),
        P("gx", "gy"),
        P("gx", "gy"),
        P(("gx", "gy"), None, None, None),
        P("snap", None, "gx", "gy"),
    )
    out_specs = (P(("gx", "gy"), None, None, None), P("snap", None, "gx", "gy"))
    return jax.shard_map(shards, mesh=mesh, in_specs=in_specs, out_specs=out_specs, check_vma=False)
```

```python
import functools

import jax
import jax.numpy as jnp
from jax import lax
from jax.experimental import pallas as pl
from jax.experimental.pallas import tpu as pltpu
from jax.sharding import PartitionSpec as P

AB = 128
NSPEC = 3
OFFSETS = ((-1, -1), (-1, 0), (-1, 1), (0, -1), (0, 1), (1, -1), (1, 0), (1, 1))
NG = 12
NP = 24
HIGH = lax.Precision.HIGHEST
F32 = jnp.float32


def lanes_of(shape):
    return lax.broadcasted_iota(jnp.int32, shape, 1)


def subs_of(shape):
    return lax.broadcasted_iota(jnp.int32, shape, 0)


def lane_slot(slot, k):
    return slot // 3, (slot % 3) * 36 + 2 * k


def own_slot(slot, k):
    return slot // 5, (slot % 5) * 24 + 2 * (4 * (k // 6) + k % 6 - 1)


OWN = [k for k in range(18) if 0 < k % 6 < 5]


def pack_columns(tile_at, slots, columns, where, ks):
    pair = lanes_of((8, 128)) // 2
    packed = [jnp.zeros((8, 128), F32) for _ in range(columns.shape[0] // 8)]
    for slot in slots:
        for k in ks:
            t, at = where(slot, k)
            packed[t] = jnp.where(pair == at // 2, pltpu.roll(tile_at(slot, k), (at + 1) % 128, 1), packed[t])
    for t, value in enumerate(packed):
        columns[pl.ds(8 * t, 8), :] = value


def merge_edges(even, near, far):
    lane = lanes_of((8, 128))
    left, right = jnp.where(even, far, near), jnp.where(even, near, far)
    return jnp.where((lane & 1) == 0, pltpu.roll(right, 127, 1), pltpu.roll(left, 1, 1))


def edge_tiles(even, slots, far_ref, near_ref):
    edges = {}
    for t in sorted({lane_slot(slot, 0)[0] for slot in slots}):
        rows = pl.ds(8 * t, 8)
        edges[t] = merge_edges(even, near_ref[rows, :], far_ref[rows, :])

    def edge(slot, k):
        t, at = lane_slot(slot, k)
        return pltpu.roll(edges[t], 127 - at, 1)

    return edge


def merged_edge(own, above, below):
    def edge(slot, k):
        x = k % 6 - 1
        source, base, at_k = (above, 240, k + 4) if x < 0 else (below, 240, k - 4) if x > 3 else (own, 0, k)
        t, at = own_slot(slot, at_k)
        step = (127 - at) % 128
        return pltpu.roll(source[pl.ds(base + 8 * t, 8), :], step, 1)

    return edge


def spread_columns(edge, tile_at, slots, shift_ref, height):
    lane = lanes_of((8, 128))
    for k in range(18):
        for place, slot in enumerate(slots):
            values = tile_at(slot, k)
            outside = edge(slot, k)
            base = k * height + 8 * place
            shift_ref[pl.ds(base, 8), :] = jnp.where(lane == 0, outside, pltpu.roll(values, 1, 1))
            shift_ref[pl.ds(18 * height + base, 8), :] = values
            shift_ref[pl.ds(36 * height + base, 8), :] = jnp.where(lane == 127, outside, pltpu.roll(values, 127, 1))


def first_kernel(disp_in, vec_in, disp, vec, columns, low, high, sems):
    copies = [pltpu.make_async_copy(disp_in, disp, sems.at[0]), pltpu.make_async_copy(vec_in, vec, sems.at[1])]
    for copy in copies:
        copy.start()
    for copy in copies:
        copy.wait()
    disp_tile, vec_tile = natural_tile(disp, None, None, 0), natural_tile(vec, None, None, 0)
    pack_columns(
        lambda slot, k: disp_tile(slot, k) if slot < 2 else vec_tile(slot - 2, k), range(10), columns, own_slot, OWN
    )
    for out, x in ((low, 0), (high, 3)):
        out[pl.ds(0, 48), :] = disp[pl.ds(x, 48, stride=4), :]
        out[pl.ds(48, 192), :] = vec[pl.ds(x, 192, stride=4), :]


def edges_kernel(par, near, far, low, high, own, low_out, high_out):
    for t in range(2):
        rows = pl.ds(8 * t, 8)
        merged = merge_edges(par[0] == 0, near[rows, :], far[rows, :])
        own[rows, :] = merged
        low_out[pl.ds(240 + 8 * t, 8), :] = merged
        high_out[pl.ds(240 + 8 * t, 8), :] = merged
    low_out[pl.ds(0, 240), :] = low[...]
    high_out[pl.ds(0, 240), :] = high[...]


def load_kernel(
    load_in, nbr_in, species, block_of, precond_in,
    load, nbr, group, precond, masks, members, kind, block, sems,
):
    pairs = [(species, kind), (block_of, block), (load_in, load), (nbr_in, nbr), (precond_in, precond)]
    copies = [pltpu.make_async_copy(source, out, sems.at[i]) for i, (source, out) in enumerate(pairs)]
    for copy in copies:
        copy.start()
    for copy in copies:
        copy.wait()
    group[...] = block[...] * NSPEC + kind[...]
    which = subs_of((128, 128)) & 15
    p_row, o_col = subs_of((NP, 8)), lanes_of((NP, 8))
    repeat = ((p_row >= 3 * o_col) & (p_row < 3 * o_col + 3)).astype(jnp.bfloat16)
    for x in range(4):
        mask = nbr[pl.ds(x, 8, stride=4), :].astype(F32).astype(jnp.bfloat16)
        masks[pl.ds(NP * x, NP), :] = jnp.dot(repeat, mask, preferred_element_type=F32)
        members[:, pl.ds(128 * x, 128)] = (which == group[pl.ds(x, 1), :]).astype(F32).astype(jnp.bfloat16)


def natural_tile(source, above, below, base):
    def tile(place, k):
        b, x = k // 6, k % 6 - 1
        if 0 <= x < 4:
            return source[pl.ds(12 * 8 * place + 4 * b + x, 8, stride=12), :]
        return (above if x < 0 else below)[pl.ds(base + 24 * place + b, 8, stride=3), :]

    return tile


def term_tile(low, mid, high, above, below):
    def tile(place, k):
        b, x = k // 6, k % 6 - 1
        if x in (1, 2):
            return mid[pl.ds((2 * b + x - 1) * 64 + 8 * place, 8), :]
        return {-1: above, 0: low, 3: high, 4: below}[x][pl.ds(b * 64 + 8 * place, 8), :]

    return tile


def term_columns_kernel(low, mid, high, above, below, columns):
    pack_columns(term_tile(low, mid, high, above, below), range(8), columns, lane_slot, range(18))


def fold_rows(tiles, sub):
    for bit in (1, 2, 4):
        low = (sub & bit) == 0
        tiles = [
            jnp.where(low, tiles[2 * i], tiles[2 * i + 1])
            + pltpu.roll(jnp.where(low, tiles[2 * i + 1], tiles[2 * i]), bit, 0)
            for i in range(len(tiles) // 2)
        ]
    return tiles[0]


def fold_lanes(tiles, eighth):
    for bit in (1, 2, 4):
        low = (eighth & bit) == 0
        tiles = [
            jnp.where(low, tiles[2 * i], tiles[2 * i + 1])
            + pltpu.roll(jnp.where(low, tiles[2 * i + 1], tiles[2 * i]), 16 * bit, 1)
            for i in range(len(tiles) // 2)
        ]
    return tiles[0]


PAIRS = [(q, p) for q in range(NP) for p in range(q, NP + 3)]
PAIR_AT = {pair: i for i, pair in enumerate(PAIRS)}
BLOCKS = [(i, j) for i in range(3) for j in range(i, 3)]
PAYLOAD = 64
CHUNK = 62


def gram_kernel(copies, own, disp, forces, nbr, group, above, below, out, shift, feats, sums):
    edge = merged_edge(own, above, below)
    spread_columns(edge, natural_tile(disp, above, below, 0), range(2), shift, 16)
    for x in range(4):
        for o, (dx, dy) in enumerate(OFFSETS):
            mask = nbr[pl.ds(4 * o + x, 1), :].astype(F32)
            for b in range(3):
                moved = shift[pl.ds(((dy + 1) * 18 + 6 * b + x + dx + 1) * 16, 16), :]
                center = shift[pl.ds((18 + 6 * b + x + 1) * 16, 16), :]
                feats[pl.ds((3 * o + b) * 64 + x, 16, stride=4), :] = (moved - center) * mask
        for a in range(3):
            feats[pl.ds((NP + a) * 64 + x, 16, stride=4), :] = forces[pl.ds(4 * a + x, 16, stride=12), :]
    for q in range(NP):
        left = feats[pl.ds(q * 64, 64), :].reshape(8, 8, 128)
        for p in range(q, NP + 3):
            right = feats[pl.ds(p * 64, 64), :].reshape(8, 8, 128)
            sums[pl.ds(PAIR_AT[q, p] * 8, 8), :] = jnp.sum(left * right, axis=0)
    which = subs_of((16, 128))
    members = jnp.concatenate([(which == group[pl.ds(x % 4, 1), :]).astype(F32) for x in range(8)], axis=0)
    members = members.astype(jnp.bfloat16)
    members = jnp.concatenate([members, members], axis=1)
    sub, eighth = subs_of((8, 128)), lanes_of((8, 128)) // 16
    diagonal = (sub == eighth).astype(F32)
    for c in range(len(PAIRS) // CHUNK):
        at = pl.ds(c * CHUNK * 8, CHUNK * 8)
        value = sums[at, :]
        high = value.astype(jnp.bfloat16)
        low = (value - high.astype(F32)).astype(jnp.bfloat16)
        by_group = lax.dot_general(
            jnp.concatenate([high, low], axis=1), members, (((1,), (1,)), ((), ())), preferred_element_type=F32
        )
        sums[at, :] = (by_group.reshape(CHUNK, 8, 128) * diagonal[None]).reshape(CHUNK * 8, 128)

    def column(fixed, block):
        pairs = [(min(fixed, 8 * block + r), max(fixed, 8 * block + r)) for r in range(8)]
        return fold_rows([sums[pl.ds(PAIR_AT[pair] * 8, 8), :] for pair in pairs], sub)

    packed = [fold_lanes([column(8 * i + r, j) for r in range(8)], eighth) for i, j in BLOCKS]
    sides = [column(NP + a, block) for a in range(3) for block in range(3)] + [jnp.zeros((8, 128), F32)] * 7
    packed += [fold_lanes(sides[:8], eighth), fold_lanes(sides[8:], eighth)]
    for i, value in enumerate(packed):
        for copy in range(copies):
            out[pl.ds(copy * PAYLOAD + 8 * i, 8), :] = value


def apply_operator(shift, weights, lattice_rows, emit):
    for x in lattice_rows:
        total = [None] * 3
        for b in range(3):
            center = shift[pl.ds((18 + 6 * b + x + 1) * 64, 64), :]
            for o, (dx, dy) in enumerate(OFFSETS):
                moved = shift[pl.ds(((dy + 1) * 18 + 6 * b + x + dx + 1) * 64, 64), :]
                differ = center - moved
                for a in range(3):
                    term = differ * weights[pl.ds(72 * x + 24 * a + 3 * o + b, 1), :]
                    total[a] = term if total[a] is None else total[a] + term
        for a in range(3):
            emit(a, x, total[a])


def fit_kernel(
    copies, scale, own, sums, precond, vec, masks, members, above, below,
    theta, weights, low_out, high_out, shift,
):
    sub, eighth = subs_of((8, 128)), lanes_of((8, 128)) // 16

    def total(i):
        value = sums[pl.ds(8 * i, 8), :]
        for copy in range(1, copies):
            value = value + sums[pl.ds(copy * PAYLOAD + 8 * i, 8), :]
        return value * scale

    def spread(value, k):
        value = jnp.where(eighth == k, value, 0.0)
        for step in (16, 32, 64):
            value = value + pltpu.roll(value, step, 1)
        return value

    sides = [spread(total(6 + i // 8), i % 8) for i in range(9)]
    rhs = []
    for block in range(3):
        value = jnp.where(eighth == 0, sides[block], 0.0)
        for a in (1, 2):
            value = jnp.where(eighth == a, sides[3 * a + block], value)
        rhs.append(value)
    of_group = lanes_of((NP, 128)) & 15

    def solve(right):
        every = jnp.dot(precond[...], right, precision=HIGH, preferred_element_type=F32)
        result = every[0:NP]
        for g in range(1, NG):
            result = jnp.where(of_group == g, every[g * NP : (g + 1) * NP], result)
        return result

    first = solve(jnp.concatenate(rhs, axis=0))
    part = [first[8 * i : 8 * i + 8] for i in range(3)]
    remain = list(rhs)
    for m, (i, j) in enumerate(BLOCKS):
        value = total(m)
        tiles = [spread(value, r) for r in range(8)]
        for r in range(8):
            remain[j] = remain[j] - tiles[r] * part[i][r : r + 1, :]
        if i != j:
            remain[i] = remain[i] - fold_rows([tiles[r] * part[j] for r in range(8)], sub)
    fitted = first + solve(jnp.concatenate(remain, axis=0))
    theta[...] = fitted

    of_part = lanes_of((NP, 128)) // 16
    stacked = jnp.concatenate(
        [jnp.where((of_part == a) & (of_group < NG), fitted, 0.0) for a in range(3)], axis=0
    )
    by_atom = None
    for _ in range(3):
        piece = stacked.astype(jnp.bfloat16)
        stacked = stacked - piece.astype(F32)
        term = jnp.dot(piece, members[...], preferred_element_type=F32)
        by_atom = term if by_atom is None else by_atom + term
    for x in range(4):
        mask = masks[pl.ds(NP * x, NP), :]
        weights[pl.ds(72 * x, 72), :] = by_atom[:, 128 * x : 128 * x + 128] * jnp.concatenate([mask] * 3, axis=0)

    tile = natural_tile(vec, above, below, 48)
    edge = merged_edge(own, above, below)
    spread_columns(edge, lambda slot, k: tile(slot - 2, k), range(2, 10), shift, 64)

    def emit(a, x, value):
        (high_out if x else low_out)[pl.ds(64 * a, 64), :] = value

    apply_operator(shift, weights, (0, 3), emit)


def middle_kernel(shift, weights, theta, mid, constants):
    def emit(a, x, value):
        mid[pl.ds((2 * a + x - 1) * 64, 64), :] = value

    apply_operator(shift, weights, (1, 2), emit)
    row, lane = subs_of((36, 128)), lanes_of((36, 128))
    which = row >> 2
    kind = (which >= 3).astype(jnp.int32) + (which >= 6).astype(jnp.int32)
    pick = (lane == 16 * (which - 3 * kind) + 3 * (row & 3) + kind).astype(F32)
    picked = lax.dot_general(
        pick, theta[...], (((1,), (1,)), ((), ())), precision=HIGH, preferred_element_type=F32
    )
    for i in range(9):
        constants[i] = picked[4 * i : 4 * i + 4]


def inner_kernel(low, mid, high, above, below, weights, vec, out, shift):
    empty = jnp.zeros((8, 128), F32)
    spread_columns(lambda slot, k: empty, term_tile(low, mid, high, above, below), range(8), shift, 64)

    def emit(a, x, value):
        out[pl.ds((4 * a + x) * 64, 64), :] = 2.0 * value - vec[pl.ds(4 * a + x, 64, stride=12), :]

    apply_operator(shift, weights, range(4), emit)


def outer_kernel(par, inner, near, far, weights, out, edges, result, sems):
    edge = edge_tiles(par[0] == 0, range(8), far, near)
    lane = lanes_of((1, 128))
    copies = []
    for half in range(2):
        for k in range(18):
            for slot in range(4 * half, 4 * half + 4):
                edges[pl.ds(64 * k + 8 * slot, 8), :] = edge(slot, k)
        for x in range(4):
            total = [inner[pl.ds((4 * a + x) * 64 + 32 * half, 32), :] for a in range(3)]
            for b in range(3):
                for dx in (-1, 0, 1):
                    outside = edges[pl.ds(64 * (6 * b + x + dx + 1) + 32 * half, 32), :]
                    for a in range(3):
                        base = 72 * x + 24 * a + b
                        left = weights[pl.ds(base + 3 * OFFSETS.index((dx, -1)), 1), :]
                        right = weights[pl.ds(base + 3 * OFFSETS.index((dx, 1)), 1), :]
                        weight = jnp.where(lane == 0, 2.0 * left, jnp.where(lane == 127, 2.0 * right, 0.0))
                        total[a] = total[a] - outside * weight
            for a in range(3):
                result[pl.ds(384 * half + 4 * a + x, 32, stride=12), :] = total[a]
        rows = pl.ds(384 * half, 384)
        copies.append(pltpu.make_async_copy(result.at[rows, :], out.at[rows, :], sems.at[half]))
        copies[half].start()
    for copy in copies:
        copy.wait()


IN_SMEM = pl.BlockSpec(memory_space=pltpu.SMEM)
IN_VMEM = pl.BlockSpec(memory_space=pltpu.VMEM)
IN_HBM = pl.BlockSpec(memory_space=pltpu.HBM)


def call(kernel, name, ins, outs, scratch=(), flops=0, out_spec=IN_VMEM):
    outs = [jax.ShapeDtypeStruct((rows, 128), F32) if isinstance(rows, int) else rows for rows in outs]
    return pl.pallas_call(
        kernel,
        name=name,
        in_specs=ins,
        out_specs=[out_spec] * len(outs),
        out_shape=outs,
        scratch_shapes=[pltpu.VMEM((rows, 128), F32) if isinstance(rows, int) else rows for rows in scratch],
        compiler_params=pltpu.CompilerParams(vmem_limit_bytes=40 << 20),
        cost_estimate=pl.CostEstimate(flops=flops, bytes_accessed=1 << 20, transcendentals=0),
    )


def along(value, axis, step):
    n = lax.axis_size(axis)
    return lax.ppermute(value, axis, [(i, (i + step) % n) for i in range(n)])


def from_both(columns):
    n = lax.axis_size("gy")
    near = lax.ppermute(columns, "gy", [(i, i ^ 1) for i in range(n)])
    pairs = [(i, (i + 1) % n) for i in range(1, n, 2)]
    far = lax.ppermute(columns, "gy", pairs + [(j, i) for i, j in pairs])
    return near, far


def shards(displacements, forces, neighbours, species, block_of, precond, vectors):
    snap = lax.axis_size("snap")
    scale = 1.0 / (displacements.shape[0] * snap * AB)
    par = (lax.axis_index("gy") % 2).astype(jnp.int32).reshape(1)

    def in_hbm(*values):
        return [pltpu.with_memory_space_constraint(value, pltpu.HBM) for value in values]

    disp, vec, columns, low, high = call(
        first_kernel, "first", [IN_HBM] * 2, (192, 768, 16, 240, 240), (pltpu.SemaphoreType.DMA((2,)),)
    )(*in_hbm(displacements.reshape(-1, 128), vectors.reshape(-1, 128)))
    near, far = from_both(columns)
    small = pltpu.VMEM((4, 128), jnp.int32)
    load, nbr, group, inverses, masks, members = call(
        load_kernel,
        "load",
        [IN_HBM] * 5,
        (
            192,
            jax.ShapeDtypeStruct((32, 128), jnp.int32),
            jax.ShapeDtypeStruct((4, 128), jnp.int32),
            jax.ShapeDtypeStruct((NG * NP, NP), F32),
            4 * NP,
            jax.ShapeDtypeStruct((128, 512), jnp.bfloat16),
        ),
        (small, small, pltpu.SemaphoreType.DMA((5,))),
        flops=1 << 24,
    )(
        *in_hbm(
            forces.reshape(-1, 128),
            neighbours.reshape(-1, 128),
            species,
            block_of,
            precond.reshape(NG * NP, NP),
        )
    )
    own, low, high = call(edges_kernel, "edges", [IN_SMEM] + [IN_VMEM] * 4, (16, 256, 256))(par, near, far, low, high)
    above, below = along(high, "gx", 1), along(low, "gx", -1)
    (part,) = call(
        functools.partial(gram_kernel, snap),
        "gram",
        [IN_VMEM] * 7,
        (snap * PAYLOAD,),
        (54 * 16, 27 * 64, len(PAIRS) * 8),
    )(own, disp, load, nbr, group, above, below)
    part = lax.all_to_all(part, "snap", 0, 0, tiled=True)
    theta, weights, low, high, shift = call(
        functools.partial(fit_kernel, snap, scale),
        "fit",
        [IN_VMEM] * 8,
        (NP, 288, 192, 192, 54 * 64),
    )(own, part, inverses, vec, masks, members, above, below)
    above, below = along(high, "gx", 1), along(low, "gx", -1)
    mid, constants = call(
        middle_kernel,
        "middle",
        [IN_VMEM] * 3,
        (384, jax.ShapeDtypeStruct((9, 4, NP), F32)),
        flops=1 << 24,
    )(shift, weights, theta)
    (columns,) = call(term_columns_kernel, "term_columns", [IN_VMEM] * 5, (24,))(low, mid, high, above, below)
    near, far = from_both(columns)
    (inner,) = call(inner_kernel, "inner", [IN_VMEM] * 7, (768,), (54 * 64,), flops=1 << 25)(
        low, mid, high, above, below, weights, vec
    )
    (result,) = call(
        outer_kernel,
        "outer",
        [IN_SMEM] + [IN_VMEM] * 4,
        (768,),
        (18 * 64, 768, pltpu.SemaphoreType.DMA((2,))),
        out_spec=IN_HBM,
    )(
        par, inner, near, far, weights
    )

    constants = constants.reshape(NSPEC, 3, precond.shape[0], NP).transpose(2, 0, 3, 1)
    return (constants, result.reshape(vectors.shape))


def solution(mesh):
    in_specs = (
        P("snap", None, "gx", "gy"),
        P("snap", None, "gx", "gy"),
        P(None, "gx", "gy"),
        P("gx", "gy"),
        P("gx", "gy"),
        P(("gx", "gy"), None, None, None),
        P("snap", None, "gx", "gy"),
    )
    out_specs = (P(("gx", "gy"), None, None, None), P("snap", None, "gx", "gy"))
    return jax.shard_map(shards, mesh=mesh, in_specs=in_specs, out_specs=out_specs, check_vma=False)
```

```python
import functools

import jax
import jax.numpy as jnp
from jax import lax
from jax.experimental import pallas as pl
from jax.experimental.pallas import tpu as pltpu
from jax.sharding import PartitionSpec as P

AB = 128
NSPEC = 3
OFFSETS = ((-1, -1), (-1, 0), (-1, 1), (0, -1), (0, 1), (1, -1), (1, 0), (1, 1))
NG = 12
NP = 24
HIGH = lax.Precision.HIGHEST
F32 = jnp.float32


def lanes_of(shape):
    return lax.broadcasted_iota(jnp.int32, shape, 1)


def subs_of(shape):
    return lax.broadcasted_iota(jnp.int32, shape, 0)


def lane_slot(slot, k):
    return slot // 3, (slot % 3) * 36 + 2 * k


def own_slot(slot, k):
    return slot // 5, (slot % 5) * 24 + 2 * (4 * (k // 6) + k % 6 - 1)


OWN = [k for k in range(18) if 0 < k % 6 < 5]


def pack_columns(tile_at, slots, columns, where, ks):
    pair = lanes_of((8, 128)) // 2
    packed = [jnp.zeros((8, 128), F32) for _ in range(columns.shape[0] // 8)]
    for slot in slots:
        for k in ks:
            t, at = where(slot, k)
            packed[t] = jnp.where(pair == at // 2, pltpu.roll(tile_at(slot, k), (at + 1) % 128, 1), packed[t])
    for t, value in enumerate(packed):
        columns[pl.ds(8 * t, 8), :] = value


def merge_edges(even, near, far):
    lane = lanes_of((8, 128))
    left, right = jnp.where(even, far, near), jnp.where(even, near, far)
    return jnp.where((lane & 1) == 0, pltpu.roll(right, 127, 1), pltpu.roll(left, 1, 1))


def edge_tiles(even, slots, far_ref, near_ref):
    edges = {}
    for t in sorted({lane_slot(slot, 0)[0] for slot in slots}):
        rows = pl.ds(8 * t, 8)
        edges[t] = merge_edges(even, near_ref[rows, :], far_ref[rows, :])

    def edge(slot, k):
        t, at = lane_slot(slot, k)
        return pltpu.roll(edges[t], 127 - at, 1)

    return edge


def merged_edge(own, above, below):
    def edge(slot, k):
        x = k % 6 - 1
        source, base, at_k = (above, 240, k + 4) if x < 0 else (below, 240, k - 4) if x > 3 else (own, 0, k)
        t, at = own_slot(slot, at_k)
        step = (127 - at) % 128
        return pltpu.roll(source[pl.ds(base + 8 * t, 8), :], step, 1)

    return edge


def spread_columns(edge, tile_at, slots, shift_ref, height):
    lane = lanes_of((8, 128))
    for k in range(18):
        for place, slot in enumerate(slots):
            values = tile_at(slot, k)
            outside = edge(slot, k)
            base = k * height + 8 * place
            shift_ref[pl.ds(base, 8), :] = jnp.where(lane == 0, outside, pltpu.roll(values, 1, 1))
            shift_ref[pl.ds(18 * height + base, 8), :] = values
            shift_ref[pl.ds(36 * height + base, 8), :] = jnp.where(lane == 127, outside, pltpu.roll(values, 127, 1))


def first_kernel(disp_in, vec_in, disp, vec, columns, low, high, sems):
    copies = [pltpu.make_async_copy(disp_in, disp, sems.at[0])]
    for part in range(4):
        rows = pl.ds(192 * part, 192)
        copies.append(pltpu.make_async_copy(vec_in.at[rows, :], vec.at[rows, :], sems.at[1 + part]))
    for copy in copies:
        copy.start()
    disp_tile, vec_tile = natural_tile(disp, None, None, 0), natural_tile(vec, None, None, 0)

    def tile(slot, k):
        if k == OWN[0] and slot % 2 == 0:
            copies[slot // 2].wait()
        return disp_tile(slot, k) if slot < 2 else vec_tile(slot - 2, k)

    pack_columns(tile, range(10), columns, own_slot, OWN)
    for out, x in ((low, 0), (high, 3)):
        out[pl.ds(0, 48), :] = disp[pl.ds(x, 48, stride=4), :]
        out[pl.ds(48, 192), :] = vec[pl.ds(x, 192, stride=4), :]


def edges_kernel(par, near, far, low, high, own, low_out, high_out):
    for t in range(2):
        rows = pl.ds(8 * t, 8)
        merged = merge_edges(par[0] == 0, near[rows, :], far[rows, :])
        own[rows, :] = merged
        low_out[pl.ds(240 + 8 * t, 8), :] = merged
        high_out[pl.ds(240 + 8 * t, 8), :] = merged
    low_out[pl.ds(0, 240), :] = low[...]
    high_out[pl.ds(0, 240), :] = high[...]


def load_kernel(
    load_in, nbr_in, species, block_of, precond_in,
    load, nbr, group, precond, masks, members, kind, block, sems,
):
    pairs = [(species, kind), (block_of, block), (load_in, load), (nbr_in, nbr), (precond_in, precond)]
    copies = [pltpu.make_async_copy(source, out, sems.at[i]) for i, (source, out) in enumerate(pairs)]
    for copy in copies:
        copy.start()
    for copy in copies:
        copy.wait()
    group[...] = block[...] * NSPEC + kind[...]
    which = subs_of((128, 128)) & 15
    p_row, o_col = subs_of((NP, 8)), lanes_of((NP, 8))
    repeat = ((p_row >= 3 * o_col) & (p_row < 3 * o_col + 3)).astype(jnp.bfloat16)
    for x in range(4):
        mask = nbr[pl.ds(x, 8, stride=4), :].astype(F32).astype(jnp.bfloat16)
        masks[pl.ds(NP * x, NP), :] = jnp.dot(repeat, mask, preferred_element_type=F32)
        members[:, pl.ds(128 * x, 128)] = (which == group[pl.ds(x, 1), :]).astype(F32).astype(jnp.bfloat16)


def natural_tile(source, above, below, base):
    def tile(place, k):
        b, x = k // 6, k % 6 - 1
        if 0 <= x < 4:
            return source[pl.ds(12 * 8 * place + 4 * b + x, 8, stride=12), :]
        return (above if x < 0 else below)[pl.ds(base + 24 * place + b, 8, stride=3), :]

    return tile


def term_tile(low, mid, high, above, below):
    def tile(place, k):
        b, x = k // 6, k % 6 - 1
        if x in (1, 2):
            return mid[pl.ds((2 * b + x - 1) * 64 + 8 * place, 8), :]
        return {-1: above, 0: low, 3: high, 4: below}[x][pl.ds(b * 64 + 8 * place, 8), :]

    return tile


def term_columns_kernel(low, mid, high, above, below, columns):
    pack_columns(term_tile(low, mid, high, above, below), range(8), columns, lane_slot, range(18))


def fold_rows(tiles, sub):
    for bit in (1, 2, 4):
        low = (sub & bit) == 0
        tiles = [
            jnp.where(low, tiles[2 * i], tiles[2 * i + 1])
            + pltpu.roll(jnp.where(low, tiles[2 * i + 1], tiles[2 * i]), bit, 0)
            for i in range(len(tiles) // 2)
        ]
    return tiles[0]


def fold_lanes(tiles, eighth):
    for bit in (1, 2, 4):
        low = (eighth & bit) == 0
        tiles = [
            jnp.where(low, tiles[2 * i], tiles[2 * i + 1])
            + pltpu.roll(jnp.where(low, tiles[2 * i + 1], tiles[2 * i]), 16 * bit, 1)
            for i in range(len(tiles) // 2)
        ]
    return tiles[0]


PAIRS = [(q, p) for q in range(NP) for p in range(q, NP + 3)]
PAIR_AT = {pair: i for i, pair in enumerate(PAIRS)}
BLOCKS = [(i, j) for i in range(3) for j in range(i, 3)]
PAYLOAD = 64
CHUNK = 62


def gram_kernel(copies, own, disp, forces, nbr, group, above, below, out, shift, feats, sums):
    edge = merged_edge(own, above, below)
    spread_columns(edge, natural_tile(disp, above, below, 0), range(2), shift, 16)
    for x in range(4):
        for o, (dx, dy) in enumerate(OFFSETS):
            mask = nbr[pl.ds(4 * o + x, 1), :].astype(F32)
            for b in range(3):
                moved = shift[pl.ds(((dy + 1) * 18 + 6 * b + x + dx + 1) * 16, 16), :]
                center = shift[pl.ds((18 + 6 * b + x + 1) * 16, 16), :]
                feats[pl.ds((3 * o + b) * 64 + x, 16, stride=4), :] = (moved - center) * mask
        for a in range(3):
            feats[pl.ds((NP + a) * 64 + x, 16, stride=4), :] = forces[pl.ds(4 * a + x, 16, stride=12), :]
    for q in range(NP):
        left = feats[pl.ds(q * 64, 64), :].reshape(8, 8, 128)
        for p in range(q, NP + 3):
            right = feats[pl.ds(p * 64, 64), :].reshape(8, 8, 128)
            sums[pl.ds(PAIR_AT[q, p] * 8, 8), :] = jnp.sum(left * right, axis=0)
    which = subs_of((16, 128))
    members = jnp.concatenate([(which == group[pl.ds(x % 4, 1), :]).astype(F32) for x in range(8)], axis=0)
    members = members.astype(jnp.bfloat16)
    members = jnp.concatenate([members, members], axis=1)
    sub, eighth = subs_of((8, 128)), lanes_of((8, 128)) // 16
    diagonal = (sub == eighth).astype(F32)
    for c in range(len(PAIRS) // CHUNK):
        at = pl.ds(c * CHUNK * 8, CHUNK * 8)
        value = sums[at, :]
        high = value.astype(jnp.bfloat16)
        low = (value - high.astype(F32)).astype(jnp.bfloat16)
        by_group = lax.dot_general(
            jnp.concatenate([high, low], axis=1), members, (((1,), (1,)), ((), ())), preferred_element_type=F32
        )
        sums[at, :] = (by_group.reshape(CHUNK, 8, 128) * diagonal[None]).reshape(CHUNK * 8, 128)

    def column(fixed, block):
        pairs = [(min(fixed, 8 * block + r), max(fixed, 8 * block + r)) for r in range(8)]
        return fold_rows([sums[pl.ds(PAIR_AT[pair] * 8, 8), :] for pair in pairs], sub)

    packed = [fold_lanes([column(8 * i + r, j) for r in range(8)], eighth) for i, j in BLOCKS]
    sides = [column(NP + a, block) for a in range(3) for block in range(3)] + [jnp.zeros((8, 128), F32)] * 7
    packed += [fold_lanes(sides[:8], eighth), fold_lanes(sides[8:], eighth)]
    for i, value in enumerate(packed):
        for copy in range(copies):
            out[pl.ds(copy * PAYLOAD + 8 * i, 8), :] = value


def apply_operator(shift, weights, lattice_rows, emit):
    for x in lattice_rows:
        total = [None] * 3
        for b in range(3):
            center = shift[pl.ds((18 + 6 * b + x + 1) * 64, 64), :]
            for o, (dx, dy) in enumerate(OFFSETS):
                moved = shift[pl.ds(((dy + 1) * 18 + 6 * b + x + dx + 1) * 64, 64), :]
                differ = center - moved
                for a in range(3):
                    term = differ * weights[pl.ds(72 * x + 24 * a + 3 * o + b, 1), :]
                    total[a] = term if total[a] is None else total[a] + term
        for a in range(3):
            emit(a, x, total[a])


def fit_kernel(
    copies, scale, own, sums, precond, vec, masks, members, above, below,
    theta, weights, low_out, high_out, shift,
):
    sub, eighth = subs_of((8, 128)), lanes_of((8, 128)) // 16

    def total(i):
        value = sums[pl.ds(8 * i, 8), :]
        for copy in range(1, copies):
            value = value + sums[pl.ds(copy * PAYLOAD + 8 * i, 8), :]
        return value * scale

    def spread(value, k):
        value = jnp.where(eighth == k, value, 0.0)
        for step in (16, 32, 64):
            value = value + pltpu.roll(value, step, 1)
        return value

    sides = [spread(total(6 + i // 8), i % 8) for i in range(9)]
    rhs = []
    for block in range(3):
        value = jnp.where(eighth == 0, sides[block], 0.0)
        for a in (1, 2):
            value = jnp.where(eighth == a, sides[3 * a + block], value)
        rhs.append(value)
    of_group = lanes_of((NP, 128)) & 15

    def solve(right):
        every = jnp.dot(precond[...], right, precision=HIGH, preferred_element_type=F32)
        result = every[0:NP]
        for g in range(1, NG):
            result = jnp.where(of_group == g, every[g * NP : (g + 1) * NP], result)
        return result

    first = solve(jnp.concatenate(rhs, axis=0))
    part = [first[8 * i : 8 * i + 8] for i in range(3)]
    remain = list(rhs)
    for m, (i, j) in enumerate(BLOCKS):
        value = total(m)
        tiles = [spread(value, r) for r in range(8)]
        for r in range(8):
            remain[j] = remain[j] - tiles[r] * part[i][r : r + 1, :]
        if i != j:
            remain[i] = remain[i] - fold_rows([tiles[r] * part[j] for r in range(8)], sub)
    fitted = first + solve(jnp.concatenate(remain, axis=0))
    theta[...] = fitted

    of_part = lanes_of((NP, 128)) // 16
    stacked = jnp.concatenate(
        [jnp.where((of_part == a) & (of_group < NG), fitted, 0.0) for a in range(3)], axis=0
    )
    by_atom = None
    for _ in range(3):
        piece = stacked.astype(jnp.bfloat16)
        stacked = stacked - piece.astype(F32)
        term = jnp.dot(piece, members[...], preferred_element_type=F32)
        by_atom = term if by_atom is None else by_atom + term
    for x in range(4):
        mask = masks[pl.ds(NP * x, NP), :]
        weights[pl.ds(72 * x, 72), :] = by_atom[:, 128 * x : 128 * x + 128] * jnp.concatenate([mask] * 3, axis=0)

    tile = natural_tile(vec, above, below, 48)
    edge = merged_edge(own, above, below)
    spread_columns(edge, lambda slot, k: tile(slot - 2, k), range(2, 10), shift, 64)

    def emit(a, x, value):
        (high_out if x else low_out)[pl.ds(64 * a, 64), :] = value

    apply_operator(shift, weights, (0, 3), emit)


def middle_kernel(shift, weights, theta, mid, constants):
    def emit(a, x, value):
        mid[pl.ds((2 * a + x - 1) * 64, 64), :] = value

    apply_operator(shift, weights, (1, 2), emit)
    row, lane = subs_of((36, 128)), lanes_of((36, 128))
    which = row >> 2
    kind = (which >= 3).astype(jnp.int32) + (which >= 6).astype(jnp.int32)
    pick = (lane == 16 * (which - 3 * kind) + 3 * (row & 3) + kind).astype(F32)
    picked = lax.dot_general(
        pick, theta[...], (((1,), (1,)), ((), ())), precision=HIGH, preferred_element_type=F32
    )
    for i in range(9):
        constants[i] = picked[4 * i : 4 * i + 4]


def inner_kernel(low, mid, high, above, below, weights, vec, out, outside, shift):
    lane = lanes_of((1, 128))
    for x in range(4):
        for a in range(3):
            for b in range(3):
                for dx in (-1, 0, 1):
                    base = 72 * x + 24 * a + b
                    left = weights[pl.ds(base + 3 * OFFSETS.index((dx, -1)), 1), :]
                    right = weights[pl.ds(base + 3 * OFFSETS.index((dx, 1)), 1), :]
                    outside[pl.ds(27 * x + 9 * a + 3 * b + dx + 1, 1), :] = jnp.where(
                        lane == 0, 2.0 * left, jnp.where(lane == 127, 2.0 * right, 0.0)
                    )
    empty = jnp.zeros((8, 128), F32)
    spread_columns(lambda slot, k: empty, term_tile(low, mid, high, above, below), range(8), shift, 64)

    def emit(a, x, value):
        out[pl.ds((4 * a + x) * 64, 64), :] = 2.0 * value - vec[pl.ds(4 * a + x, 64, stride=12), :]

    apply_operator(shift, weights, range(4), emit)


def outer_kernel(par, inner, near, far, weights, out, edges, result, sems):
    edge = edge_tiles(par[0] == 0, range(8), far, near)
    copies = []
    for half in range(2):
        for k in range(18):
            for slot in range(4 * half, 4 * half + 4):
                edges[pl.ds(64 * k + 8 * slot, 8), :] = edge(slot, k)
        for x in range(4):
            total = [inner[pl.ds((4 * a + x) * 64 + 32 * half, 32), :] for a in range(3)]
            for b in range(3):
                for dx in (-1, 0, 1):
                    outside = edges[pl.ds(64 * (6 * b + x + dx + 1) + 32 * half, 32), :]
                    for a in range(3):
                        weight = weights[pl.ds(27 * x + 9 * a + 3 * b + dx + 1, 1), :]
                        total[a] = total[a] - outside * weight
            for a in range(3):
                result[pl.ds(384 * half + 4 * a + x, 32, stride=12), :] = total[a]
        rows = pl.ds(384 * half, 384)
        copies.append(pltpu.make_async_copy(result.at[rows, :], out.at[rows, :], sems.at[half]))
        copies[half].start()
    for copy in copies:
        copy.wait()


IN_SMEM = pl.BlockSpec(memory_space=pltpu.SMEM)
IN_VMEM = pl.BlockSpec(memory_space=pltpu.VMEM)
IN_HBM = pl.BlockSpec(memory_space=pltpu.HBM)


def call(kernel, name, ins, outs, scratch=(), flops=0, out_spec=IN_VMEM):
    outs = [jax.ShapeDtypeStruct((rows, 128), F32) if isinstance(rows, int) else rows for rows in outs]
    return pl.pallas_call(
        kernel,
        name=name,
        in_specs=ins,
        out_specs=[out_spec] * len(outs),
        out_shape=outs,
        scratch_shapes=[pltpu.VMEM((rows, 128), F32) if isinstance(rows, int) else rows for rows in scratch],
        compiler_params=pltpu.CompilerParams(vmem_limit_bytes=40 << 20),
        cost_estimate=pl.CostEstimate(flops=flops, bytes_accessed=1 << 20, transcendentals=0),
    )


def along(value, axis, step):
    n = lax.axis_size(axis)
    return lax.ppermute(value, axis, [(i, (i + step) % n) for i in range(n)])


def from_both(columns):
    n = lax.axis_size("gy")
    near = lax.ppermute(columns, "gy", [(i, i ^ 1) for i in range(n)])
    pairs = [(i, (i + 1) % n) for i in range(1, n, 2)]
    far = lax.ppermute(columns, "gy", pairs + [(j, i) for i, j in pairs])
    return near, far


def shards(displacements, forces, neighbours, species, block_of, precond, vectors):
    snap = lax.axis_size("snap")
    scale = 1.0 / (displacements.shape[0] * snap * AB)
    par = (lax.axis_index("gy") % 2).astype(jnp.int32).reshape(1)

    def in_hbm(*values):
        return [pltpu.with_memory_space_constraint(value, pltpu.HBM) for value in values]

    disp, vec, columns, low, high = call(
        first_kernel, "first", [IN_HBM] * 2, (192, 768, 16, 240, 240), (pltpu.SemaphoreType.DMA((5,)),)
    )(*in_hbm(displacements.reshape(-1, 128), vectors.reshape(-1, 128)))
    near, far = from_both(columns)
    small = pltpu.VMEM((4, 128), jnp.int32)
    load, nbr, group, inverses, masks, members = call(
        load_kernel,
        "load",
        [IN_HBM] * 5,
        (
            192,
            jax.ShapeDtypeStruct((32, 128), jnp.int32),
            jax.ShapeDtypeStruct((4, 128), jnp.int32),
            jax.ShapeDtypeStruct((NG * NP, NP), F32),
            4 * NP,
            jax.ShapeDtypeStruct((128, 512), jnp.bfloat16),
        ),
        (small, small, pltpu.SemaphoreType.DMA((5,))),
        flops=1 << 24,
    )(
        *in_hbm(
            forces.reshape(-1, 128),
            neighbours.reshape(-1, 128),
            species,
            block_of,
            precond.reshape(NG * NP, NP),
        )
    )
    own, low, high = call(edges_kernel, "edges", [IN_SMEM] + [IN_VMEM] * 4, (16, 256, 256))(par, near, far, low, high)
    above, below = along(high, "gx", 1), along(low, "gx", -1)
    (part,) = call(
        functools.partial(gram_kernel, snap),
        "gram",
        [IN_VMEM] * 7,
        (snap * PAYLOAD,),
        (54 * 16, 27 * 64, len(PAIRS) * 8),
    )(own, disp, load, nbr, group, above, below)
    part = lax.all_to_all(part, "snap", 0, 0, tiled=True)
    theta, weights, low, high, shift = call(
        functools.partial(fit_kernel, snap, scale),
        "fit",
        [IN_VMEM] * 8,
        (NP, 288, 192, 192, 54 * 64),
    )(own, part, inverses, vec, masks, members, above, below)
    above, below = along(high, "gx", 1), along(low, "gx", -1)
    mid, constants = call(
        middle_kernel,
        "middle",
        [IN_VMEM] * 3,
        (384, jax.ShapeDtypeStruct((9, 4, NP), F32)),
        flops=1 << 24,
    )(shift, weights, theta)
    (columns,) = call(term_columns_kernel, "term_columns", [IN_VMEM] * 5, (24,))(low, mid, high, above, below)
    near, far = from_both(columns)
    inner, outside = call(inner_kernel, "inner", [IN_VMEM] * 7, (768, 108), (54 * 64,), flops=1 << 25)(
        low, mid, high, above, below, weights, vec
    )
    (result,) = call(
        outer_kernel,
        "outer",
        [IN_SMEM] + [IN_VMEM] * 4,
        (768,),
        (18 * 64, 768, pltpu.SemaphoreType.DMA((2,))),
        out_spec=IN_HBM,
    )(
        par, inner, near, far, outside
    )

    constants = constants.reshape(NSPEC, 3, precond.shape[0], NP).transpose(2, 0, 3, 1)
    return (constants, result.reshape(vectors.shape))


def solution(mesh):
    in_specs = (
        P("snap", None, "gx", "gy"),
        P("snap", None, "gx", "gy"),
        P(None, "gx", "gy"),
        P("gx", "gy"),
        P("gx", "gy"),
        P(("gx", "gy"), None, None, None),
        P("snap", None, "gx", "gy"),
    )
    out_specs = (P(("gx", "gy"), None, None, None), P("snap", None, "gx", "gy"))
    return jax.shard_map(shards, mesh=mesh, in_specs=in_specs, out_specs=out_specs, check_vma=False)
```

```python
import functools

import jax
import jax.numpy as jnp
from jax import lax
from jax.experimental import pallas as pl
from jax.experimental.pallas import tpu as pltpu
from jax.sharding import PartitionSpec as P

AB = 128
NSPEC = 3
OFFSETS = ((-1, -1), (-1, 0), (-1, 1), (0, -1), (0, 1), (1, -1), (1, 0), (1, 1))
NG = 12
NP = 24
HIGH = lax.Precision.HIGHEST
F32 = jnp.float32


def lanes_of(shape):
    return lax.broadcasted_iota(jnp.int32, shape, 1)


def subs_of(shape):
    return lax.broadcasted_iota(jnp.int32, shape, 0)


def lane_slot(slot, k):
    return slot // 3, (slot % 3) * 36 + 2 * k


def own_slot(slot, k):
    return slot // 5, (slot % 5) * 24 + 2 * (4 * (k // 6) + k % 6 - 1)


OWN = [k for k in range(18) if 0 < k % 6 < 5]


def pack_columns(tile_at, slots, columns, where, ks):
    pair = lanes_of((8, 128)) // 2
    packed = [jnp.zeros((8, 128), F32) for _ in range(columns.shape[0] // 8)]
    for slot in slots:
        for k in ks:
            t, at = where(slot, k)
            packed[t] = jnp.where(pair == at // 2, pltpu.roll(tile_at(slot, k), (at + 1) % 128, 1), packed[t])
    for t, value in enumerate(packed):
        columns[pl.ds(8 * t, 8), :] = value


def merge_edges(even, near, far):
    lane = lanes_of((8, 128))
    left, right = jnp.where(even, far, near), jnp.where(even, near, far)
    return jnp.where((lane & 1) == 0, pltpu.roll(right, 127, 1), pltpu.roll(left, 1, 1))


def edge_tiles(even, slots, far_ref, near_ref):
    edges = {}
    for t in sorted({lane_slot(slot, 0)[0] for slot in slots}):
        rows = pl.ds(8 * t, 8)
        edges[t] = merge_edges(even, near_ref[rows, :], far_ref[rows, :])

    def edge(slot, k):
        t, at = lane_slot(slot, k)
        return pltpu.roll(edges[t], 127 - at, 1)

    return edge


def merged_edge(own, above, below):
    def edge(slot, k):
        x = k % 6 - 1
        source, base, at_k = (above, 240, k + 4) if x < 0 else (below, 240, k - 4) if x > 3 else (own, 0, k)
        t, at = own_slot(slot, at_k)
        step = (127 - at) % 128
        return pltpu.roll(source[pl.ds(base + 8 * t, 8), :], step, 1)

    return edge


def spread_columns(edge, tile_at, slots, shift_ref, height):
    lane = lanes_of((8, 128))
    for k in range(18):
        for place, slot in enumerate(slots):
            values = tile_at(slot, k)
            outside = edge(slot, k)
            base = k * height + 8 * place
            shift_ref[pl.ds(base, 8), :] = jnp.where(lane == 0, outside, pltpu.roll(values, 1, 1))
            shift_ref[pl.ds(18 * height + base, 8), :] = values
            shift_ref[pl.ds(36 * height + base, 8), :] = jnp.where(lane == 127, outside, pltpu.roll(values, 127, 1))


def first_kernel(disp_in, vec_in, disp, vec, columns, low, high, sems):
    copies = [pltpu.make_async_copy(disp_in, disp, sems.at[0])]
    for part in range(4):
        rows = pl.ds(192 * part, 192)
        copies.append(pltpu.make_async_copy(vec_in.at[rows, :], vec.at[rows, :], sems.at[1 + part]))
    for copy in copies:
        copy.start()
    disp_tile, vec_tile = natural_tile(disp, None, None, 0), natural_tile(vec, None, None, 0)

    def tile(slot, k):
        if k == OWN[0] and slot % 2 == 0:
            copies[slot // 2].wait()
        return disp_tile(slot, k) if slot < 2 else vec_tile(slot - 2, k)

    pack_columns(tile, range(10), columns, own_slot, OWN)
    for out, x in ((low, 0), (high, 3)):
        out[pl.ds(0, 48), :] = disp[pl.ds(x, 48, stride=4), :]
        out[pl.ds(48, 192), :] = vec[pl.ds(x, 192, stride=4), :]


def edges_kernel(par, near, far, low, high, own, low_out, high_out):
    for t in range(2):
        rows = pl.ds(8 * t, 8)
        merged = merge_edges(par[0] == 0, near[rows, :], far[rows, :])
        own[rows, :] = merged
        low_out[pl.ds(240 + 8 * t, 8), :] = merged
        high_out[pl.ds(240 + 8 * t, 8), :] = merged
    low_out[pl.ds(0, 240), :] = low[...]
    high_out[pl.ds(0, 240), :] = high[...]


def load_kernel(
    load_in, nbr_in, species, block_of, precond_in,
    load, nbr, group, precond, masks, members, kind, block, sems,
):
    pairs = [(species, kind), (block_of, block), (load_in, load), (nbr_in, nbr), (precond_in, precond)]
    copies = [pltpu.make_async_copy(source, out, sems.at[i]) for i, (source, out) in enumerate(pairs)]
    for copy in copies:
        copy.start()
    for copy in copies:
        copy.wait()
    group[...] = block[...] * NSPEC + kind[...]
    which = subs_of((128, 128)) & 15
    p_row, o_col = subs_of((NP, 8)), lanes_of((NP, 8))
    repeat = ((p_row >= 3 * o_col) & (p_row < 3 * o_col + 3)).astype(jnp.bfloat16)
    for x in range(4):
        mask = nbr[pl.ds(x, 8, stride=4), :].astype(F32).astype(jnp.bfloat16)
        masks[pl.ds(NP * x, NP), :] = jnp.dot(repeat, mask, preferred_element_type=F32)
        members[:, pl.ds(128 * x, 128)] = (which == group[pl.ds(x, 1), :]).astype(F32).astype(jnp.bfloat16)


def natural_tile(source, above, below, base):
    def tile(place, k):
        b, x = k // 6, k % 6 - 1
        if 0 <= x < 4:
            return source[pl.ds(12 * 8 * place + 4 * b + x, 8, stride=12), :]
        return (above if x < 0 else below)[pl.ds(base + 24 * place + b, 8, stride=3), :]

    return tile


def term_tile(low, mid, high, above, below):
    def tile(place, k):
        b, x = k // 6, k % 6 - 1
        if x in (1, 2):
            return mid[pl.ds((2 * b + x - 1) * 64 + 8 * place, 8), :]
        return {-1: above, 0: low, 3: high, 4: below}[x][pl.ds(b * 64 + 8 * place, 8), :]

    return tile


def term_columns_kernel(low, mid, high, above, below, columns):
    pack_columns(term_tile(low, mid, high, above, below), range(8), columns, lane_slot, range(18))


def fold_rows(tiles, sub):
    for bit in (1, 2, 4):
        low = (sub & bit) == 0
        tiles = [
            jnp.where(low, tiles[2 * i], tiles[2 * i + 1])
            + pltpu.roll(jnp.where(low, tiles[2 * i + 1], tiles[2 * i]), bit, 0)
            for i in range(len(tiles) // 2)
        ]
    return tiles[0]


def fold_lanes(tiles, eighth):
    for bit in (1, 2, 4):
        low = (eighth & bit) == 0
        tiles = [
            jnp.where(low, tiles[2 * i], tiles[2 * i + 1])
            + pltpu.roll(jnp.where(low, tiles[2 * i + 1], tiles[2 * i]), 16 * bit, 1)
            for i in range(len(tiles) // 2)
        ]
    return tiles[0]


PAIRS = [(q, p) for q in range(NP) for p in range(q, NP + 3)]
PAIR_AT = {pair: i for i, pair in enumerate(PAIRS)}
BLOCKS = [(i, j) for i in range(3) for j in range(i + 1, 3)]
PAYLOAD = 48
CHUNK = 62


def gram_kernel(copies, own, disp, forces, nbr, group, above, below, out, shift, feats, sums):
    edge = merged_edge(own, above, below)
    spread_columns(edge, natural_tile(disp, above, below, 0), range(2), shift, 16)
    for x in range(4):
        for o, (dx, dy) in enumerate(OFFSETS):
            mask = nbr[pl.ds(4 * o + x, 1), :].astype(F32)
            for b in range(3):
                moved = shift[pl.ds(((dy + 1) * 18 + 6 * b + x + dx + 1) * 16, 16), :]
                center = shift[pl.ds((18 + 6 * b + x + 1) * 16, 16), :]
                feats[pl.ds((3 * o + b) * 64 + x, 16, stride=4), :] = (moved - center) * mask
        for a in range(3):
            feats[pl.ds((NP + a) * 64 + x, 16, stride=4), :] = forces[pl.ds(4 * a + x, 16, stride=12), :]
    for q in range(NP):
        left = feats[pl.ds(q * 64, 64), :].reshape(8, 8, 128)
        for p in range(q, NP + 3):
            right = feats[pl.ds(p * 64, 64), :].reshape(8, 8, 128)
            sums[pl.ds(PAIR_AT[q, p] * 8, 8), :] = jnp.sum(left * right, axis=0)
    which = subs_of((16, 128))
    members = jnp.concatenate([(which == group[pl.ds(x % 4, 1), :]).astype(F32) for x in range(8)], axis=0)
    members = members.astype(jnp.bfloat16)
    members = jnp.concatenate([members, members], axis=1)
    sub, eighth = subs_of((8, 128)), lanes_of((8, 128)) // 16
    diagonal = (sub == eighth).astype(F32)
    for c in range(len(PAIRS) // CHUNK):
        at = pl.ds(c * CHUNK * 8, CHUNK * 8)
        value = sums[at, :]
        high = value.astype(jnp.bfloat16)
        low = (value - high.astype(F32)).astype(jnp.bfloat16)
        by_group = lax.dot_general(
            jnp.concatenate([high, low], axis=1), members, (((1,), (1,)), ((), ())), preferred_element_type=F32
        )
        sums[at, :] = (by_group.reshape(CHUNK, 8, 128) * diagonal[None]).reshape(CHUNK * 8, 128)

    def column(fixed, block):
        pairs = [(min(fixed, 8 * block + r), max(fixed, 8 * block + r)) for r in range(8)]
        return fold_rows([sums[pl.ds(PAIR_AT[pair] * 8, 8), :] for pair in pairs], sub)

    def lower(block, q):
        pairs = [(q, r) if r >= q else (8 - q, 8 - q + r) for r in range(8)]
        at = [PAIR_AT[8 * block + i, 8 * block + j] for i, j in pairs]
        return fold_rows([sums[pl.ds(8 * i, 8), :] for i in at], sub)

    tiles = [column(8 * i + r, j) for i, j in BLOCKS for r in range(8)]
    tiles += [lower(block, q) for block in range(3) for q in range(5)]
    tiles += [column(NP + a, block) for a in range(3) for block in range(3)]
    packed = [fold_lanes(tiles[8 * m : 8 * m + 8], eighth) for m in range(6)]
    for i, value in enumerate(packed):
        for copy in range(copies):
            out[pl.ds(copy * PAYLOAD + 8 * i, 8), :] = value


def apply_operator(shift, weights, lattice_rows, emit):
    for x in lattice_rows:
        total = [None] * 3
        for b in range(3):
            center = shift[pl.ds((18 + 6 * b + x + 1) * 64, 64), :]
            for o, (dx, dy) in enumerate(OFFSETS):
                moved = shift[pl.ds(((dy + 1) * 18 + 6 * b + x + dx + 1) * 64, 64), :]
                differ = center - moved
                for a in range(3):
                    term = differ * weights[pl.ds(72 * x + 24 * a + 3 * o + b, 1), :]
                    total[a] = term if total[a] is None else total[a] + term
        for a in range(3):
            emit(a, x, total[a])


def fit_kernel(
    copies, scale, own, sums, precond, vec, masks, members, above, below,
    theta, weights, low_out, high_out, shift,
):
    sub, eighth = subs_of((8, 128)), lanes_of((8, 128)) // 16

    def total(i):
        value = sums[pl.ds(8 * i, 8), :]
        for copy in range(1, copies):
            value = value + sums[pl.ds(copy * PAYLOAD + 8 * i, 8), :]
        return value * scale

    def spread(value, k):
        value = jnp.where(eighth == k, value, 0.0)
        for step in (16, 32, 64):
            value = value + pltpu.roll(value, step, 1)
        return value

    totals = [total(m) for m in range(6)]

    def tile_of(i):
        return spread(totals[i // 8], i % 8)

    sides = [tile_of(39 + i) for i in range(9)]
    rhs = []
    for block in range(3):
        value = jnp.where(eighth == 0, sides[block], 0.0)
        for a in (1, 2):
            value = jnp.where(eighth == a, sides[3 * a + block], value)
        rhs.append(value)
    of_group = lanes_of((NP, 128)) & 15

    def solve(right):
        every = jnp.dot(precond[...], right, precision=HIGH, preferred_element_type=F32)
        result = every[0:NP]
        for g in range(1, NG):
            result = jnp.where(of_group == g, every[g * NP : (g + 1) * NP], result)
        return result

    first = solve(jnp.concatenate(rhs, axis=0))
    part = [first[8 * i : 8 * i + 8] for i in range(3)]
    remain = list(rhs)
    for m, (i, j) in enumerate(BLOCKS):
        tiles = [tile_of(8 * m + r) for r in range(8)]
        for r in range(8):
            remain[j] = remain[j] - tiles[r] * part[i][r : r + 1, :]
        remain[i] = remain[i] - fold_rows([tiles[r] * part[j] for r in range(8)], sub)
    for i in range(3):
        mixed = [tile_of(24 + 5 * i + q) for q in range(5)]
        lower = mixed + [pltpu.roll(mixed[8 - q], q, 0) for q in (5, 6, 7)]
        for q in range(8):
            remain[i] = remain[i] - jnp.where(sub >= q, lower[q], 0.0) * part[i][q : q + 1, :]
        remain[i] = remain[i] - fold_rows([jnp.where(sub > q, lower[q], 0.0) * part[i] for q in range(8)], sub)
    fitted = first + solve(jnp.concatenate(remain, axis=0))
    theta[...] = fitted

    of_part = lanes_of((NP, 128)) // 16
    stacked = jnp.concatenate(
        [jnp.where((of_part == a) & (of_group < NG), fitted, 0.0) for a in range(3)], axis=0
    )
    by_atom = None
    for _ in range(3):
        piece = stacked.astype(jnp.bfloat16)
        stacked = stacked - piece.astype(F32)
        term = jnp.dot(piece, members[...], preferred_element_type=F32)
        by_atom = term if by_atom is None else by_atom + term
    for x in range(4):
        mask = masks[pl.ds(NP * x, NP), :]
        weights[pl.ds(72 * x, 72), :] = by_atom[:, 128 * x : 128 * x + 128] * jnp.concatenate([mask] * 3, axis=0)

    tile = natural_tile(vec, above, below, 48)
    edge = merged_edge(own, above, below)
    spread_columns(edge, lambda slot, k: tile(slot - 2, k), range(2, 10), shift, 64)

    def emit(a, x, value):
        (high_out if x else low_out)[pl.ds(64 * a, 64), :] = value

    apply_operator(shift, weights, (0, 3), emit)


def middle_kernel(shift, weights, theta, mid, constants):
    def emit(a, x, value):
        mid[pl.ds((2 * a + x - 1) * 64, 64), :] = value

    apply_operator(shift, weights, (1, 2), emit)
    row, lane = subs_of((36, 128)), lanes_of((36, 128))
    which = row >> 2
    kind = (which >= 3).astype(jnp.int32) + (which >= 6).astype(jnp.int32)
    pick = (lane == 16 * (which - 3 * kind) + 3 * (row & 3) + kind).astype(F32)
    picked = lax.dot_general(
        pick, theta[...], (((1,), (1,)), ((), ())), precision=HIGH, preferred_element_type=F32
    )
    for i in range(9):
        constants[i] = picked[4 * i : 4 * i + 4]


def inner_kernel(low, mid, high, above, below, weights, vec, out, outside, shift):
    lane = lanes_of((1, 128))
    for x in range(4):
        for a in range(3):
            for b in range(3):
                for dx in (-1, 0, 1):
                    base = 72 * x + 24 * a + b
                    left = weights[pl.ds(base + 3 * OFFSETS.index((dx, -1)), 1), :]
                    right = weights[pl.ds(base + 3 * OFFSETS.index((dx, 1)), 1), :]
                    outside[pl.ds(27 * x + 9 * a + 3 * b + dx + 1, 1), :] = jnp.where(
                        lane == 0, 2.0 * left, jnp.where(lane == 127, 2.0 * right, 0.0)
                    )
    empty = jnp.zeros((8, 128), F32)
    spread_columns(lambda slot, k: empty, term_tile(low, mid, high, above, below), range(8), shift, 64)

    def emit(a, x, value):
        out[pl.ds((4 * a + x) * 64, 64), :] = 2.0 * value - vec[pl.ds(4 * a + x, 64, stride=12), :]

    apply_operator(shift, weights, range(4), emit)


def outer_kernel(par, inner, near, far, weights, out, edges, result, sems):
    edge = edge_tiles(par[0] == 0, range(8), far, near)
    copies = []
    for half in range(2):
        for k in range(18):
            for slot in range(4 * half, 4 * half + 4):
                edges[pl.ds(64 * k + 8 * slot, 8), :] = edge(slot, k)
        for x in range(4):
            total = [inner[pl.ds((4 * a + x) * 64 + 32 * half, 32), :] for a in range(3)]
            for b in range(3):
                for dx in (-1, 0, 1):
                    outside = edges[pl.ds(64 * (6 * b + x + dx + 1) + 32 * half, 32), :]
                    for a in range(3):
                        weight = weights[pl.ds(27 * x + 9 * a + 3 * b + dx + 1, 1), :]
                        total[a] = total[a] - outside * weight
            for a in range(3):
                result[pl.ds(384 * half + 4 * a + x, 32, stride=12), :] = total[a]
        rows = pl.ds(384 * half, 384)
        copies.append(pltpu.make_async_copy(result.at[rows, :], out.at[rows, :], sems.at[half]))
        copies[half].start()
    for copy in copies:
        copy.wait()


IN_SMEM = pl.BlockSpec(memory_space=pltpu.SMEM)
IN_VMEM = pl.BlockSpec(memory_space=pltpu.VMEM)
IN_HBM = pl.BlockSpec(memory_space=pltpu.HBM)


def call(kernel, name, ins, outs, scratch=(), flops=0, out_spec=IN_VMEM):
    outs = [jax.ShapeDtypeStruct((rows, 128), F32) if isinstance(rows, int) else rows for rows in outs]
    return pl.pallas_call(
        kernel,
        name=name,
        in_specs=ins,
        out_specs=[out_spec] * len(outs),
        out_shape=outs,
        scratch_shapes=[pltpu.VMEM((rows, 128), F32) if isinstance(rows, int) else rows for rows in scratch],
        compiler_params=pltpu.CompilerParams(vmem_limit_bytes=40 << 20),
        cost_estimate=pl.CostEstimate(flops=flops, bytes_accessed=1 << 20, transcendentals=0),
    )


def along(value, axis, step):
    n = lax.axis_size(axis)
    return lax.ppermute(value, axis, [(i, (i + step) % n) for i in range(n)])


def from_both(columns):
    n = lax.axis_size("gy")
    near = lax.ppermute(columns, "gy", [(i, i ^ 1) for i in range(n)])
    pairs = [(i, (i + 1) % n) for i in range(1, n, 2)]
    far = lax.ppermute(columns, "gy", pairs + [(j, i) for i, j in pairs])
    return near, far


def shards(displacements, forces, neighbours, species, block_of, precond, vectors):
    snap = lax.axis_size("snap")
    scale = 1.0 / (displacements.shape[0] * snap * AB)
    par = (lax.axis_index("gy") % 2).astype(jnp.int32).reshape(1)

    def in_hbm(*values):
        return [pltpu.with_memory_space_constraint(value, pltpu.HBM) for value in values]

    disp, vec, columns, low, high = call(
        first_kernel, "first", [IN_HBM] * 2, (192, 768, 16, 240, 240), (pltpu.SemaphoreType.DMA((5,)),)
    )(*in_hbm(displacements.reshape(-1, 128), vectors.reshape(-1, 128)))
    near, far = from_both(columns)
    small = pltpu.VMEM((4, 128), jnp.int32)
    load, nbr, group, inverses, masks, members = call(
        load_kernel,
        "load",
        [IN_HBM] * 5,
        (
            192,
            jax.ShapeDtypeStruct((32, 128), jnp.int32),
            jax.ShapeDtypeStruct((4, 128), jnp.int32),
            jax.ShapeDtypeStruct((NG * NP, NP), F32),
            4 * NP,
            jax.ShapeDtypeStruct((128, 512), jnp.bfloat16),
        ),
        (small, small, pltpu.SemaphoreType.DMA((5,))),
        flops=1 << 24,
    )(
        *in_hbm(
            forces.reshape(-1, 128),
            neighbours.reshape(-1, 128),
            species,
            block_of,
            precond.reshape(NG * NP, NP),
        )
    )
    own, low, high = call(edges_kernel, "edges", [IN_SMEM] + [IN_VMEM] * 4, (16, 256, 256))(par, near, far, low, high)
    above, below = along(high, "gx", 1), along(low, "gx", -1)
    (part,) = call(
        functools.partial(gram_kernel, snap),
        "gram",
        [IN_VMEM] * 7,
        (snap * PAYLOAD,),
        (54 * 16, 27 * 64, len(PAIRS) * 8),
    )(own, disp, load, nbr, group, above, below)
    part = lax.all_to_all(part, "snap", 0, 0, tiled=True)
    theta, weights, low, high, shift = call(
        functools.partial(fit_kernel, snap, scale),
        "fit",
        [IN_VMEM] * 8,
        (NP, 288, 192, 192, 54 * 64),
    )(own, part, inverses, vec, masks, members, above, below)
    above, below = along(high, "gx", 1), along(low, "gx", -1)
    mid, constants = call(
        middle_kernel,
        "middle",
        [IN_VMEM] * 3,
        (384, jax.ShapeDtypeStruct((9, 4, NP), F32)),
        flops=1 << 24,
    )(shift, weights, theta)
    (columns,) = call(term_columns_kernel, "term_columns", [IN_VMEM] * 5, (24,))(low, mid, high, above, below)
    near, far = from_both(columns)
    inner, outside = call(inner_kernel, "inner", [IN_VMEM] * 7, (768, 108), (54 * 64,), flops=1 << 25)(
        low, mid, high, above, below, weights, vec
    )
    (result,) = call(
        outer_kernel,
        "outer",
        [IN_SMEM] + [IN_VMEM] * 4,
        (768,),
        (18 * 64, 768, pltpu.SemaphoreType.DMA((2,))),
        out_spec=IN_HBM,
    )(
        par, inner, near, far, outside
    )

    constants = constants.reshape(NSPEC, 3, precond.shape[0], NP).transpose(2, 0, 3, 1)
    return (constants, result.reshape(vectors.shape))


def solution(mesh):
    in_specs = (
        P("snap", None, "gx", "gy"),
        P("snap", None, "gx", "gy"),
        P(None, "gx", "gy"),
        P("gx", "gy"),
        P("gx", "gy"),
        P(("gx", "gy"), None, None, None),
        P("snap", None, "gx", "gy"),
    )
    out_specs = (P(("gx", "gy"), None, None, None), P("snap", None, "gx", "gy"))
    return jax.shard_map(shards, mesh=mesh, in_specs=in_specs, out_specs=out_specs, check_vma=False)
```

```python
import functools

import jax
import jax.numpy as jnp
from jax import lax
from jax.experimental import pallas as pl
from jax.experimental.pallas import tpu as pltpu
from jax.sharding import PartitionSpec as P

AB = 128
NSPEC = 3
OFFSETS = ((-1, -1), (-1, 0), (-1, 1), (0, -1), (0, 1), (1, -1), (1, 0), (1, 1))
NG = 12
NP = 24
HIGH = lax.Precision.HIGHEST
F32 = jnp.float32


def lanes_of(shape):
    return lax.broadcasted_iota(jnp.int32, shape, 1)


def subs_of(shape):
    return lax.broadcasted_iota(jnp.int32, shape, 0)


def lane_slot(slot, k):
    return slot // 3, (slot % 3) * 36 + 2 * k


def own_slot(slot, k):
    return slot // 5, (slot % 5) * 24 + 2 * (4 * (k // 6) + k % 6 - 1)


OWN = [k for k in range(18) if 0 < k % 6 < 5]


def pack_columns(tile_at, slots, columns, where, ks):
    pair = lanes_of((8, 128)) // 2
    packed = [jnp.zeros((8, 128), F32) for _ in range(columns.shape[0] // 8)]
    for slot in slots:
        for k in ks:
            t, at = where(slot, k)
            packed[t] = jnp.where(pair == at // 2, pltpu.roll(tile_at(slot, k), (at + 1) % 128, 1), packed[t])
    for t, value in enumerate(packed):
        columns[pl.ds(8 * t, 8), :] = value


def merge_edges(even, near, far):
    lane = lanes_of((8, 128))
    left, right = jnp.where(even, far, near), jnp.where(even, near, far)
    return jnp.where((lane & 1) == 0, pltpu.roll(right, 127, 1), pltpu.roll(left, 1, 1))


def edge_tiles(even, slots, far_ref, near_ref):
    edges = {}
    for t in sorted({lane_slot(slot, 0)[0] for slot in slots}):
        rows = pl.ds(8 * t, 8)
        edges[t] = merge_edges(even, near_ref[rows, :], far_ref[rows, :])

    def edge(slot, k):
        t, at = lane_slot(slot, k)
        return pltpu.roll(edges[t], 127 - at, 1)

    return edge


def merged_edge(own, above, below):
    def edge(slot, k):
        x = k % 6 - 1
        source, base, at_k = (above, 240, k + 4) if x < 0 else (below, 240, k - 4) if x > 3 else (own, 0, k)
        t, at = own_slot(slot, at_k)
        step = (127 - at) % 128
        return pltpu.roll(source[pl.ds(base + 8 * t, 8), :], step, 1)

    return edge


def spread_columns(edge, tile_at, slots, shift_ref, height):
    lane = lanes_of((8, 128))
    for k in range(18):
        for place, slot in enumerate(slots):
            values = tile_at(slot, k)
            outside = edge(slot, k)
            base = k * height + 8 * place
            shift_ref[pl.ds(base, 8), :] = jnp.where(lane == 0, outside, pltpu.roll(values, 1, 1))
            shift_ref[pl.ds(18 * height + base, 8), :] = values
            shift_ref[pl.ds(36 * height + base, 8), :] = jnp.where(lane == 127, outside, pltpu.roll(values, 127, 1))


def first_kernel(disp_in, vec_in, disp, vec, columns, low, high, sems):
    copies = [pltpu.make_async_copy(disp_in, disp, sems.at[0]), pltpu.make_async_copy(vec_in, vec, sems.at[1])]
    for copy in copies:
        copy.start()
    for copy in copies:
        copy.wait()
    disp_tile, vec_tile = natural_tile(disp, None, None, 0), natural_tile(vec, None, None, 0)

    def tile(slot, k):
        return disp_tile(slot, k) if slot < 2 else vec_tile(slot - 2, k)

    pack_columns(tile, range(10), columns, own_slot, OWN)
    for out, x in ((low, 0), (high, 3)):
        out[pl.ds(0, 48), :] = disp[pl.ds(x, 48, stride=4), :]
        out[pl.ds(48, 192), :] = vec[pl.ds(x, 192, stride=4), :]


def edges_kernel(par, near, far, low, high, own, low_out, high_out):
    for t in range(2):
        rows = pl.ds(8 * t, 8)
        merged = merge_edges(par[0] == 0, near[rows, :], far[rows, :])
        own[rows, :] = merged
        low_out[pl.ds(240 + 8 * t, 8), :] = merged
        high_out[pl.ds(240 + 8 * t, 8), :] = merged
    low_out[pl.ds(0, 240), :] = low[...]
    high_out[pl.ds(0, 240), :] = high[...]


def load_kernel(
    load_in, nbr_in, species, block_of, precond_in,
    load, nbr, group, precond, masks, members, kind, block, sems,
):
    pairs = [(species, kind), (block_of, block), (load_in, load), (nbr_in, nbr), (precond_in, precond)]
    copies = [pltpu.make_async_copy(source, out, sems.at[i]) for i, (source, out) in enumerate(pairs)]
    for copy in copies:
        copy.start()
    for copy in copies:
        copy.wait()
    group[...] = block[...] * NSPEC + kind[...]
    which = subs_of((128, 128)) & 15
    p_row, o_col = subs_of((NP, 8)), lanes_of((NP, 8))
    repeat = ((p_row >= 3 * o_col) & (p_row < 3 * o_col + 3)).astype(jnp.bfloat16)
    for x in range(4):
        mask = nbr[pl.ds(x, 8, stride=4), :].astype(F32).astype(jnp.bfloat16)
        masks[pl.ds(NP * x, NP), :] = jnp.dot(repeat, mask, preferred_element_type=F32)
        members[:, pl.ds(128 * x, 128)] = (which == group[pl.ds(x, 1), :]).astype(F32).astype(jnp.bfloat16)


def natural_tile(source, above, below, base):
    def tile(place, k):
        b, x = k // 6, k % 6 - 1
        if 0 <= x < 4:
            return source[pl.ds(12 * 8 * place + 4 * b + x, 8, stride=12), :]
        return (above if x < 0 else below)[pl.ds(base + 24 * place + b, 8, stride=3), :]

    return tile


def term_tile(low, mid, high, above, below):
    def tile(place, k):
        b, x = k // 6, k % 6 - 1
        if x in (1, 2):
            return mid[pl.ds((2 * b + x - 1) * 64 + 8 * place, 8), :]
        return {-1: above, 0: low, 3: high, 4: below}[x][pl.ds(b * 64 + 8 * place, 8), :]

    return tile


def term_columns_kernel(low, mid, high, above, below, columns):
    pack_columns(term_tile(low, mid, high, above, below), range(8), columns, lane_slot, range(18))


def fold_rows(tiles, sub):
    for bit in (1, 2, 4):
        low = (sub & bit) == 0
        tiles = [
            jnp.where(low, tiles[2 * i], tiles[2 * i + 1])
            + pltpu.roll(jnp.where(low, tiles[2 * i + 1], tiles[2 * i]), bit, 0)
            for i in range(len(tiles) // 2)
        ]
    return tiles[0]


def fold_lanes(tiles, eighth):
    for bit in (1, 2, 4):
        low = (eighth & bit) == 0
        tiles = [
            jnp.where(low, tiles[2 * i], tiles[2 * i + 1])
            + pltpu.roll(jnp.where(low, tiles[2 * i + 1], tiles[2 * i]), 16 * bit, 1)
            for i in range(len(tiles) // 2)
        ]
    return tiles[0]


PAIRS = [(q, p) for q in range(NP) for p in range(q, NP + 3)]
PAIR_AT = {pair: i for i, pair in enumerate(PAIRS)}
BLOCKS = [(i, j) for i in range(3) for j in range(i + 1, 3)]
PAYLOAD = 48
CHUNK = 62


def gram_kernel(copies, own, disp, forces, nbr, group, above, below, out, shift, feats, sums):
    edge = merged_edge(own, above, below)
    spread_columns(edge, natural_tile(disp, above, below, 0), range(2), shift, 16)
    for x in range(4):
        for o, (dx, dy) in enumerate(OFFSETS):
            mask = nbr[pl.ds(4 * o + x, 1), :].astype(F32)
            for b in range(3):
                moved = shift[pl.ds(((dy + 1) * 18 + 6 * b + x + dx + 1) * 16, 16), :]
                center = shift[pl.ds((18 + 6 * b + x + 1) * 16, 16), :]
                feats[pl.ds((3 * o + b) * 64 + x, 16, stride=4), :] = (moved - center) * mask
        for a in range(3):
            feats[pl.ds((NP + a) * 64 + x, 16, stride=4), :] = forces[pl.ds(4 * a + x, 16, stride=12), :]
    for q in range(NP):
        left = feats[pl.ds(q * 64, 64), :].reshape(8, 8, 128)
        for p in range(q, NP + 3):
            right = feats[pl.ds(p * 64, 64), :].reshape(8, 8, 128)
            sums[pl.ds(PAIR_AT[q, p] * 8, 8), :] = jnp.sum(left * right, axis=0)
    which = subs_of((16, 128))
    members = jnp.concatenate([(which == group[pl.ds(x % 4, 1), :]).astype(F32) for x in range(8)], axis=0)
    members = members.astype(jnp.bfloat16)
    members = jnp.concatenate([members, members], axis=1)
    sub, eighth = subs_of((8, 128)), lanes_of((8, 128)) // 16
    diagonal = (sub == eighth).astype(F32)
    for c in range(len(PAIRS) // CHUNK):
        at = pl.ds(c * CHUNK * 8, CHUNK * 8)
        value = sums[at, :]
        high = value.astype(jnp.bfloat16)
        low = (value - high.astype(F32)).astype(jnp.bfloat16)
        by_group = lax.dot_general(
            jnp.concatenate([high, low], axis=1), members, (((1,), (1,)), ((), ())), preferred_element_type=F32
        )
        sums[at, :] = (by_group.reshape(CHUNK, 8, 128) * diagonal[None]).reshape(CHUNK * 8, 128)

    def column(fixed, block):
        pairs = [(min(fixed, 8 * block + r), max(fixed, 8 * block + r)) for r in range(8)]
        return fold_rows([sums[pl.ds(PAIR_AT[pair] * 8, 8), :] for pair in pairs], sub)

    def lower(block, q):
        pairs = [(q, r) if r >= q else (8 - q, 8 - q + r) for r in range(8)]
        at = [PAIR_AT[8 * block + i, 8 * block + j] for i, j in pairs]
        return fold_rows([sums[pl.ds(8 * i, 8), :] for i in at], sub)

    tiles = [column(8 * i + r, j) for i, j in BLOCKS for r in range(8)]
    tiles += [lower(block, q) for block in range(3) for q in range(5)]
    tiles += [column(NP + a, block) for a in range(3) for block in range(3)]
    packed = [fold_lanes(tiles[8 * m : 8 * m + 8], eighth) for m in range(6)]
    for i, value in enumerate(packed):
        for copy in range(copies):
            out[pl.ds(copy * PAYLOAD + 8 * i, 8), :] = value


def apply_operator(shift, weights, lattice_rows, emit):
    for x in lattice_rows:
        total = [None] * 3
        for b in range(3):
            center = shift[pl.ds((18 + 6 * b + x + 1) * 64, 64), :]
            for o, (dx, dy) in enumerate(OFFSETS):
                moved = shift[pl.ds(((dy + 1) * 18 + 6 * b + x + dx + 1) * 64, 64), :]
                differ = center - moved
                for a in range(3):
                    term = differ * weights[pl.ds(72 * x + 24 * a + 3 * o + b, 1), :]
                    total[a] = term if total[a] is None else total[a] + term
        for a in range(3):
            emit(a, x, total[a])


def fit_kernel(
    copies, scale, own, sums, precond, vec, masks, members, above, below,
    theta, weights, low_out, high_out, shift,
):
    sub, eighth = subs_of((8, 128)), lanes_of((8, 128)) // 16

    def total(i):
        value = sums[pl.ds(8 * i, 8), :]
        for copy in range(1, copies):
            value = value + sums[pl.ds(copy * PAYLOAD + 8 * i, 8), :]
        return value * scale

    def spread(value, k):
        value = jnp.where(eighth == k, value, 0.0)
        for step in (16, 32, 64):
            value = value + pltpu.roll(value, step, 1)
        return value

    totals = [total(m) for m in range(6)]

    def tile_of(i):
        return spread(totals[i // 8], i % 8)

    sides = [tile_of(39 + i) for i in range(9)]
    rhs = []
    for block in range(3):
        value = jnp.where(eighth == 0, sides[block], 0.0)
        for a in (1, 2):
            value = jnp.where(eighth == a, sides[3 * a + block], value)
        rhs.append(value)
    of_group = lanes_of((NP, 128)) & 15

    def solve(right):
        every = jnp.dot(precond[...], right, precision=HIGH, preferred_element_type=F32)
        result = every[0:NP]
        for g in range(1, NG):
            result = jnp.where(of_group == g, every[g * NP : (g + 1) * NP], result)
        return result

    first = solve(jnp.concatenate(rhs, axis=0))
    part = [first[8 * i : 8 * i + 8] for i in range(3)]
    remain = list(rhs)
    for m, (i, j) in enumerate(BLOCKS):
        tiles = [tile_of(8 * m + r) for r in range(8)]
        for r in range(8):
            remain[j] = remain[j] - tiles[r] * part[i][r : r + 1, :]
        remain[i] = remain[i] - fold_rows([tiles[r] * part[j] for r in range(8)], sub)
    for i in range(3):
        mixed = [tile_of(24 + 5 * i + q) for q in range(5)]
        lower = mixed + [pltpu.roll(mixed[8 - q], q, 0) for q in (5, 6, 7)]
        for q in range(8):
            remain[i] = remain[i] - jnp.where(sub >= q, lower[q], 0.0) * part[i][q : q + 1, :]
        remain[i] = remain[i] - fold_rows([jnp.where(sub > q, lower[q], 0.0) * part[i] for q in range(8)], sub)
    fitted = first + solve(jnp.concatenate(remain, axis=0))
    theta[...] = fitted

    of_part = lanes_of((NP, 128)) // 16
    stacked = jnp.concatenate(
        [jnp.where((of_part == a) & (of_group < NG), fitted, 0.0) for a in range(3)], axis=0
    )
    by_atom = None
    for _ in range(3):
        piece = stacked.astype(jnp.bfloat16)
        stacked = stacked - piece.astype(F32)
        term = jnp.dot(piece, members[...], preferred_element_type=F32)
        by_atom = term if by_atom is None else by_atom + term
    for x in range(4):
        mask = masks[pl.ds(NP * x, NP), :]
        weights[pl.ds(72 * x, 72), :] = by_atom[:, 128 * x : 128 * x + 128] * jnp.concatenate([mask] * 3, axis=0)

    tile = natural_tile(vec, above, below, 48)
    edge = merged_edge(own, above, below)
    spread_columns(edge, lambda slot, k: tile(slot - 2, k), range(2, 10), shift, 64)

    def emit(a, x, value):
        (high_out if x else low_out)[pl.ds(64 * a, 64), :] = value

    apply_operator(shift, weights, (0, 3), emit)


def middle_kernel(shift, weights, theta, mid, constants):
    def emit(a, x, value):
        mid[pl.ds((2 * a + x - 1) * 64, 64), :] = value

    apply_operator(shift, weights, (1, 2), emit)
    row, lane = subs_of((36, 128)), lanes_of((36, 128))
    which = row >> 2
    kind = (which >= 3).astype(jnp.int32) + (which >= 6).astype(jnp.int32)
    pick = (lane == 16 * (which - 3 * kind) + 3 * (row & 3) + kind).astype(F32)
    picked = lax.dot_general(
        pick, theta[...], (((1,), (1,)), ((), ())), precision=HIGH, preferred_element_type=F32
    )
    for i in range(9):
        constants[i] = picked[4 * i : 4 * i + 4]


def inner_kernel(low, mid, high, above, below, weights, vec, out, outside, shift):
    lane = lanes_of((1, 128))
    for x in range(4):
        for a in range(3):
            for b in range(3):
                for dx in (-1, 0, 1):
                    base = 72 * x + 24 * a + b
                    left = weights[pl.ds(base + 3 * OFFSETS.index((dx, -1)), 1), :]
                    right = weights[pl.ds(base + 3 * OFFSETS.index((dx, 1)), 1), :]
                    outside[pl.ds(27 * x + 9 * a + 3 * b + dx + 1, 1), :] = jnp.where(
                        lane == 0, 2.0 * left, jnp.where(lane == 127, 2.0 * right, 0.0)
                    )
    empty = jnp.zeros((8, 128), F32)
    spread_columns(lambda slot, k: empty, term_tile(low, mid, high, above, below), range(8), shift, 64)

    def emit(a, x, value):
        out[pl.ds((4 * a + x) * 64, 64), :] = 2.0 * value - vec[pl.ds(4 * a + x, 64, stride=12), :]

    apply_operator(shift, weights, range(4), emit)


def outer_kernel(par, inner, near, far, weights, out, edges, result, sems):
    edge = edge_tiles(par[0] == 0, range(8), far, near)
    copies = []
    for half in range(2):
        for k in range(18):
            for slot in range(4 * half, 4 * half + 4):
                edges[pl.ds(64 * k + 8 * slot, 8), :] = edge(slot, k)
        for x in range(4):
            total = [inner[pl.ds((4 * a + x) * 64 + 32 * half, 32), :] for a in range(3)]
            for b in range(3):
                for dx in (-1, 0, 1):
                    outside = edges[pl.ds(64 * (6 * b + x + dx + 1) + 32 * half, 32), :]
                    for a in range(3):
                        weight = weights[pl.ds(27 * x + 9 * a + 3 * b + dx + 1, 1), :]
                        total[a] = total[a] - outside * weight
            for a in range(3):
                result[pl.ds(384 * half + 4 * a + x, 32, stride=12), :] = total[a]
        rows = pl.ds(384 * half, 384)
        copies.append(pltpu.make_async_copy(result.at[rows, :], out.at[rows, :], sems.at[half]))
        copies[half].start()
    for copy in copies:
        copy.wait()


IN_SMEM = pl.BlockSpec(memory_space=pltpu.SMEM)
IN_VMEM = pl.BlockSpec(memory_space=pltpu.VMEM)
IN_HBM = pl.BlockSpec(memory_space=pltpu.HBM)


def call(kernel, name, ins, outs, scratch=(), flops=0, out_spec=IN_VMEM):
    outs = [jax.ShapeDtypeStruct((rows, 128), F32) if isinstance(rows, int) else rows for rows in outs]
    return pl.pallas_call(
        kernel,
        name=name,
        in_specs=ins,
        out_specs=[out_spec] * len(outs),
        out_shape=outs,
        scratch_shapes=[pltpu.VMEM((rows, 128), F32) if isinstance(rows, int) else rows for rows in scratch],
        compiler_params=pltpu.CompilerParams(vmem_limit_bytes=40 << 20),
        cost_estimate=pl.CostEstimate(flops=flops, bytes_accessed=1 << 20, transcendentals=0),
    )


def along(value, axis, step):
    n = lax.axis_size(axis)
    return lax.ppermute(value, axis, [(i, (i + step) % n) for i in range(n)])


def from_both(columns):
    n = lax.axis_size("gy")
    near = lax.ppermute(columns, "gy", [(i, i ^ 1) for i in range(n)])
    pairs = [(i, (i + 1) % n) for i in range(1, n, 2)]
    far = lax.ppermute(columns, "gy", pairs + [(j, i) for i, j in pairs])
    return near, far


def shards(displacements, forces, neighbours, species, block_of, precond, vectors):
    snap = lax.axis_size("snap")
    scale = 1.0 / (displacements.shape[0] * snap * AB)
    par = (lax.axis_index("gy") % 2).astype(jnp.int32).reshape(1)

    def in_hbm(*values):
        return [pltpu.with_memory_space_constraint(value, pltpu.HBM) for value in values]

    disp, vec, columns, low, high = call(
        first_kernel, "first", [IN_HBM] * 2, (192, 768, 16, 240, 240), (pltpu.SemaphoreType.DMA((2,)),)
    )(*in_hbm(displacements.reshape(-1, 128), vectors.reshape(-1, 128)))
    near, far = from_both(columns)
    small = pltpu.VMEM((4, 128), jnp.int32)
    load, nbr, group, inverses, masks, members = call(
        load_kernel,
        "load",
        [IN_HBM] * 5,
        (
            192,
            jax.ShapeDtypeStruct((32, 128), jnp.int32),
            jax.ShapeDtypeStruct((4, 128), jnp.int32),
            jax.ShapeDtypeStruct((NG * NP, NP), F32),
            4 * NP,
            jax.ShapeDtypeStruct((128, 512), jnp.bfloat16),
        ),
        (small, small, pltpu.SemaphoreType.DMA((5,))),
        flops=1 << 24,
    )(
        *in_hbm(
            forces.reshape(-1, 128),
            neighbours.reshape(-1, 128),
            species,
            block_of,
            precond.reshape(NG * NP, NP),
        )
    )
    own, low, high = call(edges_kernel, "edges", [IN_SMEM] + [IN_VMEM] * 4, (16, 256, 256))(par, near, far, low, high)
    above, below = along(high, "gx", 1), along(low, "gx", -1)
    (part,) = call(
        functools.partial(gram_kernel, snap),
        "gram",
        [IN_VMEM] * 7,
        (snap * PAYLOAD,),
        (54 * 16, 27 * 64, len(PAIRS) * 8),
    )(own, disp, load, nbr, group, above, below)
    part = lax.all_to_all(part, "snap", 0, 0, tiled=True)
    theta, weights, low, high, shift = call(
        functools.partial(fit_kernel, snap, scale),
        "fit",
        [IN_VMEM] * 8,
        (NP, 288, 192, 192, 54 * 64),
    )(own, part, inverses, vec, masks, members, above, below)
    above, below = along(high, "gx", 1), along(low, "gx", -1)
    mid, constants = call(
        middle_kernel,
        "middle",
        [IN_VMEM] * 3,
        (384, jax.ShapeDtypeStruct((9, 4, NP), F32)),
        flops=1 << 24,
    )(shift, weights, theta)
    (columns,) = call(term_columns_kernel, "term_columns", [IN_VMEM] * 5, (24,))(low, mid, high, above, below)
    near, far = from_both(columns)
    inner, outside = call(inner_kernel, "inner", [IN_VMEM] * 7, (768, 108), (54 * 64,), flops=1 << 25)(
        low, mid, high, above, below, weights, vec
    )
    (result,) = call(
        outer_kernel,
        "outer",
        [IN_SMEM] + [IN_VMEM] * 4,
        (768,),
        (18 * 64, 768, pltpu.SemaphoreType.DMA((2,))),
        out_spec=IN_HBM,
    )(
        par, inner, near, far, outside
    )

    constants = constants.reshape(NSPEC, 3, precond.shape[0], NP).transpose(2, 0, 3, 1)
    return (constants, result.reshape(vectors.shape))


def solution(mesh):
    in_specs = (
        P("snap", None, "gx", "gy"),
        P("snap", None, "gx", "gy"),
        P(None, "gx", "gy"),
        P("gx", "gy"),
        P("gx", "gy"),
        P(("gx", "gy"), None, None, None),
        P("snap", None, "gx", "gy"),
    )
    out_specs = (P(("gx", "gy"), None, None, None), P("snap", None, "gx", "gy"))
    return jax.shard_map(shards, mesh=mesh, in_specs=in_specs, out_specs=out_specs, check_vma=False)
```
